32 devices in a mesh: row: 8 (over y, x, core), col: 4 (over z).
Axes of the slice: x: 2, y: 2, z: 4, core: 2. Of those that a mesh axis runs over, the one named last changes fastest.
Arguments:
- covariance: float32 [8192, 8192], P('row', 'col'), as said below
- innovations: float32 [512, 8, 1024], P('row', None, 'col'), may hold values from -6 to 6
- block_owner: int32 [32], replicated, may hold values from 0 to 31, as said below
- panel_index: int32 [1], replicated, may hold values from 0 to 15
Outputs:
- factor: float32 [8192, 8192], P('row', 'col')
- solved: float32 [512, 8192], P('col', 'row')
The draws below stay inside these ranges and needn't reach their ends.
Inputs may be any that keep to these rules, and one draw needn't show every extreme that they name: Storage block s holds global block block_owner[s]; every global block appears once; the storage blocks s with one value of s // 4 hold the blocks of one residue modulo 8, rising with s. `covariance`: symmetric positive definite.
All inputs are finite; a program needn't handle non-finite values.
Results may differ from the reference program's by a relative error of at most 0.0016.
Values may be sent and summed in bfloat16 or wider, within the bound.
A program may use at most 128 MiB of HBM per device.

```python
import jax
import jax.numpy as jnp
from jax import lax

B = 256
BR = 4
PANELS = 2
GROUPS = 8
ROWS_DEV = 1024
M = 8192
NBLK = 32
P_SIZE = 512


def draw_covariance(key, part):
    base_key = jax.random.fold_in(key, 11)
    load_key, nugget_key = jax.random.split(base_key)
    shared_key = jax.random.fold_in(base_key, 37)
    latent = 2 * B
    loadings = jax.random.normal(load_key, (M, latent), jnp.float32)
    weights = jax.random.uniform(shared_key, (M,), jnp.float32, 0.7, 1.3)
    nugget = jnp.exp(jax.random.uniform(nugget_key, (M,), jnp.float32, -0.6931472, 0.6931472))
    row_block = jnp.arange(M, dtype=jnp.int32) // B
    indicator = (row_block[:, None] == jnp.arange(NBLK, dtype=jnp.int32)[None, :]).astype(jnp.float32)
    shared = indicator * (1.7320508 * weights)[:, None]
    combined = jnp.concatenate([loadings * (1.0 / latent ** 0.5), shared], axis=1)
    matrix = jnp.dot(combined, combined.T, precision=lax.Precision.HIGHEST)
    matrix = 0.5 * (matrix + matrix.T)
    return matrix + jnp.diag(nugget)


def draw_block_owner(key, part):
    row_order = jax.random.permutation(jax.random.fold_in(key, 23), GROUPS)
    positions = jnp.arange(NBLK, dtype=jnp.int32)
    return (positions % BR * GROUPS + row_order[positions // BR]).astype(jnp.int32)


def level_of(key, dims, cuts, least, largest):
    gain, own = 1.0, jax.random.fold_in(key, 6)
    for position, shards_of in cuts:
        steps = jnp.exp(jax.random.uniform(jax.random.fold_in(own, position), (shards_of,), jnp.float32, least / len(cuts), largest / len(cuts)))
        gain = gain * jnp.repeat(steps, dims[position] // shards_of).reshape([-1 if axis == position else 1 for axis in range(len(dims))])
    return gain


def bell_draw(own_key, extent, deviation, reach, cuts=(), held_as=jnp.bfloat16):
    entries = deviation * jax.random.normal(own_key, extent, jnp.float32)
    if cuts:
        entries = entries * level_of(own_key, extent, cuts, -0.22, 0.18)
    return jnp.clip(entries, -reach, reach).astype(held_as)


def setup_inputs(seed: int = 0) -> dict:
    splits = jax.random.split(jax.random.key(seed), 5)
    covariance = draw_covariance(jax.random.fold_in(splits[4], 71), 0)
    innovations = bell_draw(splits[1], (P_SIZE, GROUPS, ROWS_DEV), 1.0, 6.0, ((0, 8), (2, 4)), jnp.float32)
    block_owner = draw_block_owner(jax.random.fold_in(splits[4], 71), 0)
    panel_index = jax.random.randint(splits[3], (1,), 0, NBLK // 2).astype(jnp.int32)
    return dict(covariance=covariance, innovations=innovations, block_owner=block_owner, panel_index=panel_index)


CONTRACT_LAST = (((1,), (1,)), ((), ()))

def lower_solve(factor, right_side):
    return jax.scipy.linalg.solve_triangular(factor, right_side, lower=True)

def reference(covariance, innovations, block_owner, panel_index):
    matrix_order = covariance.shape[0]
    blocks = matrix_order // B
    matrix = covariance
    solved = innovations.reshape(innovations.shape[0], matrix_order)
    row_owner = jnp.repeat(block_owner, B)
    positions = jnp.arange(blocks, dtype=jnp.int32)
    for panel_turn in range(PANELS):
        target = panel_index[0] + panel_turn
        slot_index = jnp.sum(jnp.where(block_owner == target, positions, 0)).astype(jnp.int32)
        panel_start = slot_index * B
        column = lax.dynamic_slice_in_dim(matrix, panel_start, B, 1)
        diagonal = lax.dynamic_slice_in_dim(column, panel_start, B, 0)
        factor = jnp.linalg.cholesky(diagonal)
        live_rows = row_owner > target
        panel_rows = jnp.where(live_rows[:, None], lower_solve(factor, column.T).T, 0.0)
        panel_half = panel_rows.astype(jnp.bfloat16)
        matrix = matrix - lax.dot_general(panel_half.astype(jnp.float32), panel_half.astype(jnp.float32), CONTRACT_LAST, preferred_element_type=jnp.float32)
        innovation_block = lax.dynamic_slice_in_dim(solved, panel_start, B, 1)
        whitened = lower_solve(factor, innovation_block.T).T
        solved = solved - lax.dot_general(whitened.astype(jnp.bfloat16).astype(jnp.float32), panel_half.astype(jnp.float32), CONTRACT_LAST, preferred_element_type=jnp.float32)
        solved = lax.dynamic_update_slice_in_dim(solved, whitened, panel_start, 1)
        row_block = lax.dynamic_slice_in_dim(matrix, panel_start, B, 0)
        row_block = jnp.where(live_rows[None, :], 0.0, row_block)
        matrix = lax.dynamic_update_slice_in_dim(matrix, row_block, panel_start, 0)
        column_old = lax.dynamic_slice_in_dim(matrix, panel_start, B, 1)
        column_new = jnp.where(live_rows[:, None], panel_rows, column_old)
        column_new = lax.dynamic_update_slice_in_dim(column_new, factor, panel_start, 0)
        matrix = lax.dynamic_update_slice_in_dim(matrix, column_new, panel_start, 1)
    return (matrix, solved)
```

```python
import functools

import jax
import jax.numpy as jnp
from jax import lax
from jax.experimental import pallas as pl
from jax.experimental.pallas import tpu as pltpu
from jax.sharding import PartitionSpec as P

B = 256
PANELS = 2
SUB = 64
G8 = SUB // 8
LANES = 128
TW = 2 * B // LANES
HIGHEST = lax.Precision.HIGHEST

LAST = (((1,), (1,)), ((), ()))
FIRST = (((0,), (0,)), ((), ()))
PLAIN = (((1,), (0,)), ((), ()))


def dot(a, b, dims=PLAIN, precision=None):
    return lax.dot_general(a, b, dims, precision=precision, preferred_element_type=jnp.float32)


def split_bf16(x):
    hi = x.astype(jnp.bfloat16)
    lo = (x - hi.astype(jnp.float32)).astype(jnp.bfloat16)
    return hi, lo


def dot3(a, b, dims=PLAIN):
    ah, al = split_bf16(a)
    bh, bl = split_bf16(b)
    return dot(ah, bh, dims) + (dot(ah, bl, dims) + dot(al, bh, dims))


def lanes(x):
    return jnp.broadcast_to(x, (8, LANES))


def factor_panel(s_ref, p_ref):
    sub_iota = lax.broadcasted_iota(jnp.int32, (8, LANES), 0)
    rows = [[s_ref[8 * g : 8 * g + 8, LANES * t : LANES * (t + 1)] for t in range(TW)] for g in range(G8)]
    for b in range(G8):
        c0 = 8 * b
        col = [[lanes(rows[g][0][:, c0 + j : c0 + j + 1]) for j in range(8)] for g in range(b, G8)]
        e = [[lanes(col[0][j][i : i + 1, :]) for j in range(i + 1)] for i in range(8)]
        r = []
        l = [[None] * 8 for _ in range(8)]
        for j in range(8):
            rj = lax.rsqrt(e[j][j])
            r.append(rj)
            for i in range(j + 1, 8):
                l[i][j] = e[i][j] * rj
            for i in range(j + 1, 8):
                for k in range(j + 1, i + 1):
                    e[i][k] = e[i][k] - l[i][j] * l[k][j]
        y = []
        for i in range(8):
            yi = []
            for t in range(TW):
                v = lanes(rows[b][t][i : i + 1, :])
                for j in range(i):
                    v = v - l[i][j] * y[j][t]
                yi.append(v * r[i])
            y.append(yi)
        for t in range(TW):
            u = y[0][t]
            for i in range(1, 8):
                u = jnp.where(sub_iota == i, y[i][t], u)
            p_ref[8 * b : 8 * b + 8, LANES * t : LANES * (t + 1)] = u
        for g in range(b + 1, G8):
            cs = []
            for j in range(8):
                v = col[g - b][j]
                for k in range(j):
                    v = v - l[j][k] * cs[k]
                cs.append(v * r[j])
            for t in range(TW):
                v = rows[g][t]
                for j in range(8):
                    v = v - cs[j] * y[j][t]
                rows[g][t] = v


def factor_kernel(d_ref, u_ref, z_ref, x_ref, a_ref, s_ref, p_ref):
    row_i = lax.broadcasted_iota(jnp.int32, (B, B), 0)
    col_i = lax.broadcasted_iota(jnp.int32, (B, B), 1)
    a_ref[...] = d_ref[0]

    def panel(turn, carry):
        s_ref[:, :B] = a_ref[...]
        s_ref[:, B:] = jnp.where(row_i == col_i, 1.0, 0.0)

        def step(k, carry):
            factor_panel(s_ref, p_ref)
            start = pl.multiple_of(k * SUB, SUB)
            u_ref[turn, pl.ds(start, SUB), :] = pltpu.roll(p_ref[:, :B], start, 1)
            z_ref[turn, pl.ds(start, SUB), :] = p_ref[:, B:]
            left = p_ref[:, :B]
            rolled = pltpu.roll(left, B - SUB, 1)
            lane = lax.broadcasted_iota(jnp.int32, (SUB, B), 1)
            rolled = jnp.where(lane < B - SUB, rolled, 0.0)
            upd_a = dot(rolled, rolled, FIRST, HIGHEST)
            upd_z = dot(rolled, p_ref[:, B:], FIRST, HIGHEST)
            keep = B - SUB
            old = pltpu.roll(s_ref[SUB:, :B], B - SUB, 1)
            lane2 = lax.broadcasted_iota(jnp.int32, (keep, B), 1)
            old = jnp.where(lane2 < keep, old, 0.0)
            old_z = s_ref[SUB:, B:]
            s_ref[:keep, :B] = old - upd_a[:keep]
            s_ref[:keep, B:] = old_z - upd_z[:keep]
            s_ref[keep:, :] = jnp.zeros((SUB, 2 * B), jnp.float32)
            return carry

        lax.fori_loop(0, B // SUB, step, 0)

        @pl.when(turn == 0)
        def _():
            zt = jnp.where(row_i >= col_i, z_ref[0], 0.0)
            low = dot3(d_ref[1], zt, LAST)
            half = low.astype(jnp.bfloat16)
            x_ref[...] = half
            a_ref[...] = d_ref[2] - dot(half, half, LAST)

        return carry

    lax.fori_loop(0, PANELS, panel, 0)


def factor_pair(blocks):
    return pl.pallas_call(
        factor_kernel,
        out_shape=(
            jax.ShapeDtypeStruct((PANELS, B, B), jnp.float32),
            jax.ShapeDtypeStruct((PANELS, B, B), jnp.float32),
            jax.ShapeDtypeStruct((B, B), jnp.bfloat16),
        ),
        scratch_shapes=[
            pltpu.VMEM((B, B), jnp.float32),
            pltpu.VMEM((B, 2 * B), jnp.float32),
            pltpu.VMEM((SUB, 2 * B), jnp.float32),
        ],
        cost_estimate=pl.CostEstimate(flops=100_000_000, bytes_accessed=2_000_000, transcendentals=0),
    )(blocks)


def panel_kernel(owner_ref, at_ref, cols_ref, z_ref, x_ref, out_ref, half_ref, *, blocks):
    i = pl.program_id(0)
    own = owner_ref[i]
    g = at_ref[0]
    p0 = dot3(cols_ref[:, :B], z_ref[0], LAST)
    p0 = jnp.where(own > g, p0, 0.0)
    h0 = p0.astype(jnp.bfloat16)
    c1 = cols_ref[:, B:] - dot(h0, x_ref[...], LAST)
    p1 = dot3(c1, z_ref[1], LAST)
    p1 = jnp.where(own > g + 1, p1, 0.0)
    out_ref[:, :B] = p0
    out_ref[:, B:] = p1
    half_ref[:, :B] = h0
    half_ref[:, B:] = p1.astype(jnp.bfloat16)


def solve_rows(owner, at, cols, z, x):
    rows = cols.shape[0]
    return pl.pallas_call(
        functools.partial(panel_kernel, blocks=rows // B),
        grid_spec=pltpu.PrefetchScalarGridSpec(
            num_scalar_prefetch=2,
            grid=(rows // B,),
            in_specs=[
                pl.BlockSpec((B, 2 * B), lambda i, o, a: (i, 0)),
                pl.BlockSpec((PANELS, B, B), lambda i, o, a: (0, 0, 0)),
                pl.BlockSpec((B, B), lambda i, o, a: (0, 0)),
            ],
            out_specs=[
                pl.BlockSpec((B, 2 * B), lambda i, o, a: (i, 0)),
                pl.BlockSpec((B, 2 * B), lambda i, o, a: (i, 0)),
            ],
        ),
        out_shape=(
            jax.ShapeDtypeStruct((rows, 2 * B), jnp.float32),
            jax.ShapeDtypeStruct((rows, 2 * B), jnp.bfloat16),
        ),
    )(owner, at, cols, z, x)


def update_kernel(ro_ref, co_ref, at_ref, w_ref, r_ref, z_ref, x_ref, half_ref, full_ref, f_ref, o_ref, *, rb):
    j = pl.program_id(0)
    g = at_ref[0]
    cown = co_ref[j]
    q0 = dot3(z_ref[0], r_ref[:B].astype(jnp.float32))
    q0 = jnp.where(cown > g, q0, 0.0).astype(jnp.bfloat16)
    r1 = r_ref[B:].astype(jnp.float32) - dot(x_ref[...], q0)
    q1 = dot3(z_ref[1], r1)
    q1 = jnp.where(cown > g + 1, q1, 0.0).astype(jnp.bfloat16)
    for i in range(rb):
        span = slice(i * B, (i + 1) * B)
        rown = ro_ref[i]
        new = w_ref[span] - (dot(half_ref[span, :B], q0) + dot(half_ref[span, B:], q1))
        dead = ((rown == g) & (cown > g)) | ((rown == g + 1) & (cown > g + 1))
        o_ref[span] = jnp.where(dead, 0.0, new)

        @pl.when((cown == g) & (rown > g))
        def _():
            o_ref[span] = full_ref[span, :B]

        @pl.when((cown == g) & (rown == g))
        def _():
            o_ref[span] = f_ref[0]

        @pl.when((cown == g + 1) & (rown > g + 1))
        def _():
            o_ref[span] = full_ref[span, B:]

        @pl.when((cown == g + 1) & (rown == g + 1))
        def _():
            o_ref[span] = f_ref[1]


def update(ro, co, at, w, rowpanel, z, x, half, full, factors):
    rows, cols = w.shape
    fixed2 = lambda j, a, b, c: (0, 0)
    fixed3 = lambda j, a, b, c: (0, 0, 0)
    stripe = lambda j, a, b, c: (0, j)
    return pl.pallas_call(
        functools.partial(update_kernel, rb=rows // B),
        grid_spec=pltpu.PrefetchScalarGridSpec(
            num_scalar_prefetch=3,
            grid=(cols // B,),
            in_specs=[
                pl.BlockSpec((rows, B), stripe),
                pl.BlockSpec((2 * B, B), stripe),
                pl.BlockSpec((PANELS, B, B), fixed3),
                pl.BlockSpec((B, B), fixed2),
                pl.BlockSpec((rows, 2 * B), fixed2),
                pl.BlockSpec((rows, 2 * B), fixed2),
                pl.BlockSpec((PANELS, B, B), fixed3),
            ],
            out_specs=pl.BlockSpec((rows, B), stripe),
        ),
        out_shape=jax.ShapeDtypeStruct((rows, cols), jnp.float32),
    )(ro, co, at, w, rowpanel, z, x, half, full, factors)


def locate(block_owner, target):
    positions = jnp.arange(block_owner.shape[0], dtype=jnp.int32)
    return jnp.sum(jnp.where(block_owner == target, positions, 0))


def per_device(covariance, innovations, block_owner, panel_index):
    local_rows, local_cols = covariance.shape
    row_blocks = local_rows // B
    column_blocks = local_cols // B
    r_here = lax.axis_index("row")
    c_here = lax.axis_index("col")
    g = panel_index[0]
    slots = [locate(block_owner, g + t) for t in range(PANELS)]
    rroot = [s // row_blocks for s in slots]
    croot = [s // column_blocks for s in slots]
    rstart = [s % row_blocks * B for s in slots]
    cstart = [s % column_blocks * B for s in slots]

    def block(t, u):
        tile = lax.dynamic_slice(covariance, (rstart[t], cstart[u]), (B, B))
        return jnp.where((r_here == rroot[t]) & (c_here == croot[u]), tile, 0.0)

    blocks = lax.psum(jnp.stack([block(0, 0), block(1, 0), block(1, 1)]), ("row", "col"))
    cols = jnp.concatenate(
        [
            jnp.where(c_here == croot[t], lax.dynamic_slice_in_dim(covariance, cstart[t], B, 1), 0.0)
            for t in range(PANELS)
        ],
        axis=1,
    )
    cols = lax.psum(cols, "col")
    rowpanel = jnp.concatenate(
        [
            jnp.where(r_here == rroot[t], lax.dynamic_slice_in_dim(covariance, rstart[t], B, 0), 0.0)
            for t in range(PANELS)
        ],
        axis=0,
    )
    rowpanel = lax.psum(rowpanel.astype(jnp.bfloat16), "row")

    relaid = lax.all_to_all(
        lax.all_to_all(innovations, "row", split_axis=1, concat_axis=0, tiled=True),
        "col",
        split_axis=0,
        concat_axis=2,
        tiled=True,
    )
    v = relaid.reshape(relaid.shape[0], local_rows)
    vs = jnp.concatenate(
        [
            jnp.where(r_here == rroot[t], lax.dynamic_slice_in_dim(v, rstart[t], B, 1), 0.0)
            for t in range(PANELS)
        ],
        axis=1,
    )
    vs = lax.psum(vs, "row")

    upper, z, x = factor_pair(blocks)
    tri = jnp.tril(jnp.ones((B, B), jnp.bool_))
    factors = jnp.where(tri, upper.transpose(0, 2, 1), 0.0)
    z = jnp.where(tri, z, 0.0)
    at = panel_index
    ro = lax.dynamic_slice_in_dim(block_owner, r_here * row_blocks, row_blocks)
    co = lax.dynamic_slice_in_dim(block_owner, c_here * column_blocks, column_blocks)
    full, half = solve_rows(ro, at, cols, z, x)
    w0 = dot3(vs[:, :B], z[0], LAST)
    w0h = w0.astype(jnp.bfloat16)
    w1 = dot3(vs[:, B:] - dot(w0h, x, LAST), z[1], LAST)
    w1h = w1.astype(jnp.bfloat16)
    owner_lane = jnp.repeat(ro, B)[None, :]
    wide0 = jnp.tile(w0, (1, row_blocks))
    wide1 = jnp.tile(w1, (1, row_blocks))
    v = v - dot(jnp.concatenate([w0h, w1h], axis=1), half, LAST)
    v = jnp.where(owner_lane == g, wide0, v)
    v = jnp.where(owner_lane == g + 1, wide1, v)
    matrix = update(ro, co, at, covariance, rowpanel, z, x, half, full, factors)
    return (matrix, v)


def solution(mesh):
    placed = (P("row", "col"), P("row", None, "col"), P(), P())
    return jax.shard_map(
        per_device,
        mesh=mesh,
        in_specs=placed,
        out_specs=(P("row", "col"), P("col", "row")),
        check_vma=False,
    )
```

```python
import functools

import jax
import jax.numpy as jnp
from jax import lax
from jax.experimental import pallas as pl
from jax.experimental.pallas import tpu as pltpu
from jax.sharding import PartitionSpec as P

B = 256
PANELS = 2
SUB = 64
G8 = SUB // 8
LANES = 128
TW = 2 * B // LANES
HIGHEST = lax.Precision.HIGHEST

LAST = (((1,), (1,)), ((), ()))
FIRST = (((0,), (0,)), ((), ()))
PLAIN = (((1,), (0,)), ((), ()))


def dot(a, b, dims=PLAIN, precision=None):
    return lax.dot_general(a, b, dims, precision=precision, preferred_element_type=jnp.float32)


def split_bf16(x):
    hi = x.astype(jnp.bfloat16)
    lo = (x - hi.astype(jnp.float32)).astype(jnp.bfloat16)
    return hi, lo


def dot3(a, b, dims=PLAIN):
    ah, al = split_bf16(a)
    bh, bl = split_bf16(b)
    return dot(ah, bh, dims) + (dot(ah, bl, dims) + dot(al, bh, dims))


def lanes(x):
    return jnp.broadcast_to(x, (8, LANES))


def factor_panel(s_ref, p_ref):
    sub_iota = lax.broadcasted_iota(jnp.int32, (8, LANES), 0)
    rows = [[s_ref[8 * g : 8 * g + 8, LANES * t : LANES * (t + 1)] for t in range(TW)] for g in range(G8)]
    for b in range(G8):
        c0 = 8 * b
        col = [[lanes(rows[g][0][:, c0 + j : c0 + j + 1]) for j in range(8)] for g in range(b, G8)]
        e = [[lanes(col[0][j][i : i + 1, :]) for j in range(i + 1)] for i in range(8)]
        r = []
        l = [[None] * 8 for _ in range(8)]
        for j in range(8):
            rj = lax.rsqrt(e[j][j])
            r.append(rj)
            for i in range(j + 1, 8):
                l[i][j] = e[i][j] * rj
            for i in range(j + 1, 8):
                for k in range(j + 1, i + 1):
                    e[i][k] = e[i][k] - l[i][j] * l[k][j]
        y = []
        for i in range(8):
            yi = []
            for t in range(TW):
                v = lanes(rows[b][t][i : i + 1, :])
                for j in range(i):
                    v = v - l[i][j] * y[j][t]
                yi.append(v * r[i])
            y.append(yi)
        for t in range(TW):
            u = y[0][t]
            for i in range(1, 8):
                u = jnp.where(sub_iota == i, y[i][t], u)
            p_ref[8 * b : 8 * b + 8, LANES * t : LANES * (t + 1)] = u
        for g in range(b + 1, G8):
            cs = []
            for j in range(8):
                v = col[g - b][j]
                for k in range(j):
                    v = v - l[j][k] * cs[k]
                cs.append(v * r[j])
            for t in range(TW):
                v = rows[g][t]
                for j in range(8):
                    v = v - cs[j] * y[j][t]
                rows[g][t] = v


def factor_kernel(d_ref, u_ref, z_ref, x_ref, a_ref, s_ref, p_ref):
    row_i = lax.broadcasted_iota(jnp.int32, (B, B), 0)
    col_i = lax.broadcasted_iota(jnp.int32, (B, B), 1)
    a_ref[...] = d_ref[0]

    def panel(turn, carry):
        s_ref[:, :B] = a_ref[...]
        s_ref[:, B:] = jnp.where(row_i == col_i, 1.0, 0.0)

        def step(k, carry):
            factor_panel(s_ref, p_ref)
            start = pl.multiple_of(k * SUB, SUB)
            u_ref[turn, pl.ds(start, SUB), :] = pltpu.roll(p_ref[:, :B], start, 1)
            z_ref[turn, pl.ds(start, SUB), :] = p_ref[:, B:]
            left = p_ref[:, :B]
            rolled = pltpu.roll(left, B - SUB, 1)
            lane = lax.broadcasted_iota(jnp.int32, (SUB, B), 1)
            rolled = jnp.where(lane < B - SUB, rolled, 0.0)
            upd_a = dot(rolled, rolled, FIRST, HIGHEST)
            upd_z = dot(rolled, p_ref[:, B:], FIRST, HIGHEST)
            keep = B - SUB
            old = pltpu.roll(s_ref[SUB:, :B], B - SUB, 1)
            lane2 = lax.broadcasted_iota(jnp.int32, (keep, B), 1)
            old = jnp.where(lane2 < keep, old, 0.0)
            old_z = s_ref[SUB:, B:]
            s_ref[:keep, :B] = old - upd_a[:keep]
            s_ref[:keep, B:] = old_z - upd_z[:keep]
            s_ref[keep:, :] = jnp.zeros((SUB, 2 * B), jnp.float32)
            return carry

        lax.fori_loop(0, B // SUB, step, 0)

        @pl.when(turn == 0)
        def _():
            zt = jnp.where(row_i >= col_i, z_ref[0], 0.0)
            low = dot3(d_ref[1], zt, LAST)
            half = low.astype(jnp.bfloat16)
            x_ref[...] = half
            a_ref[...] = d_ref[2] - dot(half, half, LAST)

        return carry

    lax.fori_loop(0, PANELS, panel, 0)


def factor_pair(blocks):
    return pl.pallas_call(
        factor_kernel,
        out_shape=(
            jax.ShapeDtypeStruct((PANELS, B, B), jnp.float32),
            jax.ShapeDtypeStruct((PANELS, B, B), jnp.float32),
            jax.ShapeDtypeStruct((B, B), jnp.bfloat16),
        ),
        scratch_shapes=[
            pltpu.VMEM((B, B), jnp.float32),
            pltpu.VMEM((B, 2 * B), jnp.float32),
            pltpu.VMEM((SUB, 2 * B), jnp.float32),
        ],
        cost_estimate=pl.CostEstimate(flops=100_000_000, bytes_accessed=2_000_000, transcendentals=0),
    )(blocks)


def panel_kernel(owner_ref, at_ref, cols_ref, z_ref, x_ref, out_ref, half_ref, *, blocks):
    i = pl.program_id(0)
    own = owner_ref[i]
    g = at_ref[0]
    p0 = dot3(cols_ref[:, :B], z_ref[0], LAST)
    p0 = jnp.where(own > g, p0, 0.0)
    h0 = p0.astype(jnp.bfloat16)
    c1 = cols_ref[:, B:] - dot(h0, x_ref[...], LAST)
    p1 = dot3(c1, z_ref[1], LAST)
    p1 = jnp.where(own > g + 1, p1, 0.0)
    out_ref[:, :B] = p0
    out_ref[:, B:] = p1
    half_ref[:, :B] = h0
    half_ref[:, B:] = p1.astype(jnp.bfloat16)


def solve_rows(owner, at, cols, z, x):
    rows = cols.shape[0]
    return pl.pallas_call(
        functools.partial(panel_kernel, blocks=rows // B),
        grid_spec=pltpu.PrefetchScalarGridSpec(
            num_scalar_prefetch=2,
            grid=(rows // B,),
            in_specs=[
                pl.BlockSpec((B, 2 * B), lambda i, o, a: (i, 0)),
                pl.BlockSpec((PANELS, B, B), lambda i, o, a: (0, 0, 0)),
                pl.BlockSpec((B, B), lambda i, o, a: (0, 0)),
            ],
            out_specs=[
                pl.BlockSpec((B, 2 * B), lambda i, o, a: (i, 0)),
                pl.BlockSpec((B, 2 * B), lambda i, o, a: (i, 0)),
            ],
        ),
        out_shape=(
            jax.ShapeDtypeStruct((rows, 2 * B), jnp.float32),
            jax.ShapeDtypeStruct((rows, 2 * B), jnp.bfloat16),
        ),
    )(owner, at, cols, z, x)


def update_kernel(ro_ref, co_ref, at_ref, w_ref, r_ref, z_ref, x_ref, half_ref, full_ref, f_ref, o_ref, *, rb):
    j = pl.program_id(0)
    g = at_ref[0]
    cown = co_ref[j]
    q0 = dot3(z_ref[0], r_ref[:B].astype(jnp.float32))
    q0 = jnp.where(cown > g, q0, 0.0).astype(jnp.bfloat16)
    r1 = r_ref[B:].astype(jnp.float32) - dot(x_ref[...], q0)
    q1 = dot3(z_ref[1], r1)
    q1 = jnp.where(cown > g + 1, q1, 0.0).astype(jnp.bfloat16)
    for i in range(rb):
        span = slice(i * B, (i + 1) * B)
        rown = ro_ref[i]
        new = w_ref[span] - (dot(half_ref[span, :B], q0) + dot(half_ref[span, B:], q1))
        dead = ((rown == g) & (cown > g)) | ((rown == g + 1) & (cown > g + 1))
        o_ref[span] = jnp.where(dead, 0.0, new)

        @pl.when((cown == g) & (rown > g))
        def _():
            o_ref[span] = full_ref[span, :B]

        @pl.when((cown == g) & (rown == g))
        def _():
            o_ref[span] = f_ref[0]

        @pl.when((cown == g + 1) & (rown > g + 1))
        def _():
            o_ref[span] = full_ref[span, B:]

        @pl.when((cown == g + 1) & (rown == g + 1))
        def _():
            o_ref[span] = f_ref[1]


def update(ro, co, at, w, rowpanel, z, x, half, full, factors):
    rows, cols = w.shape
    fixed2 = lambda j, a, b, c: (0, 0)
    fixed3 = lambda j, a, b, c: (0, 0, 0)
    stripe = lambda j, a, b, c: (0, j)
    return pl.pallas_call(
        functools.partial(update_kernel, rb=rows // B),
        grid_spec=pltpu.PrefetchScalarGridSpec(
            num_scalar_prefetch=3,
            grid=(cols // B,),
            in_specs=[
                pl.BlockSpec((rows, B), stripe),
                pl.BlockSpec((2 * B, B), stripe),
                pl.BlockSpec((PANELS, B, B), fixed3),
                pl.BlockSpec((B, B), fixed2),
                pl.BlockSpec((rows, 2 * B), fixed2),
                pl.BlockSpec((rows, 2 * B), fixed2),
                pl.BlockSpec((PANELS, B, B), fixed3),
            ],
            out_specs=pl.BlockSpec((rows, B), stripe),
        ),
        out_shape=jax.ShapeDtypeStruct((rows, cols), jnp.float32),
    )(ro, co, at, w, rowpanel, z, x, half, full, factors)


MESH = pl.DeviceIdType.MESH
CHUNKS = 16


def remote(src, dst, send, recv, where):
    return pltpu.make_async_remote_copy(
        src_ref=src, dst_ref=dst, send_sem=send, recv_sem=recv, device_id=where, device_id_type=MESH
    )


class RowSpread:
    def __init__(self, axis_size, in_ref, acc_ref, core_ref, hop_ref, send, recv):
        self.bits = [1 << b for b in range(1, axis_size.bit_length() - 1)]
        self.in_ref, self.acc, self.core, self.hop = in_ref, acc_ref, core_ref, hop_ref
        self.send, self.recv = send, recv
        me = lax.axis_index("row")
        self.me = me
        self.odd = lax.rem(me, 2)
        self.mate = me + 1 - 2 * self.odd
        self.rows = in_ref.shape[0]
        self.half = self.rows // 2
        self.quarter = self.rows // 4
        self.stages = len(self.bits)

    def mine(self, part=0, size=None):
        start = self.odd * self.half + part * self.quarter
        return pl.ds(pl.multiple_of(start, self.quarter), self.half if size is None else size)

    def theirs(self):
        start = (1 - self.odd) * self.half
        return pl.ds(pl.multiple_of(start, self.half), self.half)

    def partner(self, bit):
        digit = lax.rem(self.me // bit, 2)
        return {"row": self.me + bit - 2 * bit * digit}

    def first(self):
        return remote(self.in_ref.at[self.theirs()], self.core, self.send.at[0], self.recv.at[0], {"row": self.mate})

    def middle(self, stage, part):
        bit = self.bits[(stage + part) % self.stages]
        index = 1 + 2 * stage + part
        return remote(
            self.acc.at[self.mine(part, self.quarter)],
            self.hop.at[stage, part],
            self.send.at[index],
            self.recv.at[index],
            self.partner(bit),
        )

    def final(self):
        index = 1 + 2 * self.stages
        rows = self.acc.at[self.mine()]
        return remote(rows, rows, self.send.at[index], self.recv.at[index], {"row": self.mate})

    def start(self):
        self.first().start()

    def advance(self, turn):
        if turn == 0:
            self.first().wait()
            self.acc[self.mine()] = self.in_ref[self.mine()] + self.core[...]
        else:
            for part in range(2):
                self.middle(turn - 1, part).wait()
                rows = self.mine(part, self.quarter)
                self.acc[rows] = self.acc[rows] + self.hop[turn - 1, part]
        if turn < self.stages:
            for part in range(2):
                self.middle(turn, part).start()
        else:
            self.final().start()

    def finish(self):
        self.final().wait()


def spread_scratch(axis_size, shape, dtype):
    stages = axis_size.bit_length() - 2
    rows, width = shape
    count = 2 + 2 * stages
    return [
        pltpu.VMEM((rows // 2, width), dtype),
        pltpu.VMEM((stages, 2, rows // 4, width), dtype),
        pltpu.SemaphoreType.DMA((count,)),
        pltpu.SemaphoreType.DMA((count,)),
    ]


def gather_kernel(
    nr, nc, own, rowp, inn, out, rowout, v,
    rin, lin, rtx, ltx, rs, rr, ls, lr,
    core, hop, rowsend, rowrecv, vsend, vrecv, vself,
):
    r = lax.axis_index("row")
    c = lax.axis_index("col")
    size = own.shape[0] // CHUNKS
    ratio = nr // nc
    spread = RowSpread(nr, rowp, rowout, core, hop, rowsend, rowrecv)
    part_p, width = inn.shape[1], inn.shape[2]

    def chunk(q):
        return pl.ds(pl.multiple_of(q * size, size), size)

    def right(src, q):
        return remote(src.at[chunk(q)], rin.at[chunk(q)], rs.at[q], rr.at[q], {"col": c + 1})

    def left(src, q):
        return remote(src.at[chunk(q)], lin.at[chunk(q)], ls.at[q], lr.at[q], {"col": c - 1})

    spread.start()

    @pl.when(c == 0)
    def _():
        lax.fori_loop(0, CHUNKS, lambda q, k: (right(own, q).start(), k)[1], 0)
        rin[...] = jnp.zeros_like(rin)

    @pl.when(c == nc - 1)
    def _():
        lax.fori_loop(0, CHUNKS, lambda q, k: (left(own, q).start(), k)[1], 0)
        lin[...] = jnp.zeros_like(lin)

    my_col = r // ratio

    def v_copy(group):
        place = v.at[
            pl.ds(pl.multiple_of(lax.rem(r, ratio) * part_p, part_p), part_p),
            pl.ds(pl.multiple_of(c * width, width), width),
        ]
        slot = lax.rem(r, ratio) * nc + c
        return remote(inn.at[group], place, vsend.at[group], vrecv.at[slot], {"row": group, "col": my_col})

    def v_local():
        place = v.at[
            pl.ds(pl.multiple_of(lax.rem(r, ratio) * part_p, part_p), part_p),
            pl.ds(pl.multiple_of(c * width, width), width),
        ]
        return pltpu.make_async_copy(inn.at[r], place, vself)

    for shift in range(nr):
        group = lax.rem(r + shift, nr)
        if shift == 0:
            @pl.when(my_col == c)
            def _():
                v_local().start()

            @pl.when(my_col != c)
            def _():
                v_copy(group).start()
        else:
            v_copy(group).start()

    steps = CHUNKS + nc - 2

    def relay(t, carry):
        q = t - (c - 1)

        @pl.when((c > 0) & (q >= 0) & (q < CHUNKS))
        def _():
            right(own, q).wait_recv()

            @pl.when(c < nc - 1)
            def _():
                rtx[chunk(q)] = rin[chunk(q)] + own[chunk(q)]
                right(rtx, q).start()

        p = t - (nc - 2 - c)

        @pl.when((c < nc - 1) & (p >= 0) & (p < CHUNKS))
        def _():
            left(own, p).wait_recv()

            @pl.when(c > 0)
            def _():
                ltx[chunk(p)] = lin[chunk(p)] + own[chunk(p)]
                left(ltx, p).start()

        return carry

    turns = spread.stages + 1
    begin = 0
    for turn in range(turns):
        end = 1 + (steps - 1) * (turn + 1) // (turns + 1)
        lax.fori_loop(begin, end, relay, 0)
        begin = end
        spread.advance(turn)
    lax.fori_loop(begin, steps, relay, 0)

    def total(q, carry):
        out[chunk(q)] = own[chunk(q)] + (rin[chunk(q)] + lin[chunk(q)])
        return carry

    lax.fori_loop(0, CHUNKS, total, 0)

    @pl.when(c < nc - 1)
    def _():
        lax.fori_loop(0, CHUNKS, lambda q, k: (right(own, q).wait_send(), k)[1], 0)

    @pl.when(c > 0)
    def _():
        lax.fori_loop(0, CHUNKS, lambda q, k: (left(own, q).wait_send(), k)[1], 0)

    spread.finish()
    for shift in range(nr):
        group = lax.rem(r + shift, nr)
        if shift == 0:
            @pl.when(my_col == c)
            def _():
                v_local().wait()

            @pl.when(my_col != c)
            def _():
                v_copy(group).wait_send()
        else:
            v_copy(group).wait_send()
    for a in range(ratio):
        for b in range(nc):
            @pl.when((r != ratio * c + a) | (c != b))
            def _():
                place = v.at[pl.ds(a * part_p, part_p), pl.ds(b * width, width)]
                remote(
                    inn.at[0], place, vsend.at[0], vrecv.at[a * nc + b], {"row": r, "col": c}
                ).wait_recv()


def gather(nr, nc, own, rowp, inn):
    rows, width = own.shape
    vmem = pl.BlockSpec(memory_space=pltpu.VMEM)
    ratio = nr // nc
    big = pltpu.VMEM((rows, width), jnp.float32)
    sems = pltpu.SemaphoreType.DMA((CHUNKS,))
    return pl.pallas_call(
        functools.partial(gather_kernel, nr, nc),
        out_shape=(
            jax.ShapeDtypeStruct(own.shape, own.dtype),
            jax.ShapeDtypeStruct(rowp.shape, rowp.dtype),
            jax.ShapeDtypeStruct((ratio * inn.shape[1], nc * inn.shape[2]), inn.dtype),
        ),
        in_specs=[vmem] * 3,
        out_specs=(vmem,) * 3,
        scratch_shapes=[big] * 4 + [sems] * 4
        + spread_scratch(nr, rowp.shape, rowp.dtype)
        + [
            pltpu.SemaphoreType.DMA((nr,)),
            pltpu.SemaphoreType.DMA((ratio * nc,)),
            pltpu.SemaphoreType.DMA,
        ],
        compiler_params=pltpu.CompilerParams(has_side_effects=True),
    )(own, rowp, inn)


def spread_kernel(nr, in_ref, out_ref, core, hop, send, recv):
    spread = RowSpread(nr, in_ref, out_ref, core, hop, send, recv)
    spread.start()
    for turn in range(spread.stages + 1):
        spread.advance(turn)
    spread.finish()


def spread_rows(nr, value):
    vmem = pl.BlockSpec(memory_space=pltpu.VMEM)
    return pl.pallas_call(
        functools.partial(spread_kernel, nr),
        out_shape=jax.ShapeDtypeStruct(value.shape, value.dtype),
        in_specs=[vmem],
        out_specs=vmem,
        scratch_shapes=spread_scratch(nr, value.shape, value.dtype),
        compiler_params=pltpu.CompilerParams(has_side_effects=True),
    )(value)


def locate(block_owner, target):
    positions = jnp.arange(block_owner.shape[0], dtype=jnp.int32)
    return jnp.sum(jnp.where(block_owner == target, positions, 0))


def per_device(covariance, innovations, block_owner, panel_index):
    local_rows, local_cols = covariance.shape
    row_blocks = local_rows // B
    column_blocks = local_cols // B
    r_here = lax.axis_index("row")
    c_here = lax.axis_index("col")
    nr, nc = lax.axis_size("row"), lax.axis_size("col")
    g = panel_index[0]
    slots = [locate(block_owner, g + t) for t in range(PANELS)]
    rroot = [s // row_blocks for s in slots]
    croot = [s // column_blocks for s in slots]
    rstart = [s % row_blocks * B for s in slots]
    cstart = [s % column_blocks * B for s in slots]

    cols = jnp.concatenate(
        [
            jnp.where(c_here == croot[t], lax.dynamic_slice_in_dim(covariance, cstart[t], B, 1), 0.0)
            for t in range(PANELS)
        ],
        axis=1,
    )
    rowpanel = jnp.concatenate(
        [
            jnp.where(r_here == rroot[t], lax.dynamic_slice_in_dim(covariance, rstart[t], B, 0), 0.0)
            for t in range(PANELS)
        ],
        axis=0,
    )
    cols, rowpanel, v = gather(nr, nc, cols, rowpanel.astype(jnp.bfloat16), innovations.transpose(1, 0, 2))

    def pick(value, t, axis):
        tile = lax.dynamic_slice_in_dim(value, rstart[t], B, axis)
        return jnp.where(r_here == rroot[t], tile, 0.0)

    parts = [pick(cols[:, :B], 0, 0), pick(cols[:, :B], 1, 0), pick(cols[:, B:], 1, 0), pick(v, 0, 1), pick(v, 1, 1)]
    everyone = spread_rows(nr, jnp.concatenate(parts, axis=0))
    blocks = everyone[: 3 * B].reshape(3, B, B)
    vs = everyone[3 * B :].reshape(PANELS, -1, B)

    upper, z, x = factor_pair(blocks)
    tri = jnp.tril(jnp.ones((B, B), jnp.bool_))
    factors = jnp.where(tri, upper.transpose(0, 2, 1), 0.0)
    z = jnp.where(tri, z, 0.0)
    at = panel_index
    ro = lax.dynamic_slice_in_dim(block_owner, r_here * row_blocks, row_blocks)
    co = lax.dynamic_slice_in_dim(block_owner, c_here * column_blocks, column_blocks)
    full, half = solve_rows(ro, at, cols, z, x)
    w0 = dot(vs[0], z[0], LAST, HIGHEST)
    w0h = w0.astype(jnp.bfloat16)
    w1 = dot(vs[1] - dot(w0h, x, LAST), z[1], LAST, HIGHEST)
    w1h = w1.astype(jnp.bfloat16)
    owner_lane = jnp.repeat(ro, B)[None, :]
    wide0 = jnp.tile(w0, (1, row_blocks))
    wide1 = jnp.tile(w1, (1, row_blocks))
    v = v - dot(jnp.concatenate([w0h, w1h], axis=1), half, LAST)
    v = jnp.where(owner_lane == g, wide0, v)
    v = jnp.where(owner_lane == g + 1, wide1, v)
    matrix = update(ro, co, at, covariance, rowpanel, z, x, half, full, factors)
    return (matrix, v)


def solution(mesh):
    placed = (P("row", "col"), P("row", None, "col"), P(), P())
    return jax.shard_map(
        per_device,
        mesh=mesh,
        in_specs=placed,
        out_specs=(P("row", "col"), P("col", "row")),
        check_vma=False,
    )
```

```python
import functools

import jax
import jax.numpy as jnp
from jax import lax
from jax.experimental import pallas as pl
from jax.experimental.pallas import tpu as pltpu
from jax.sharding import PartitionSpec as P

B = 256
PANELS = 2
SUB = 64
G8 = SUB // 8
LANES = 128
TW = 2 * B // LANES
HIGHEST = lax.Precision.HIGHEST

LAST = (((1,), (1,)), ((), ()))
FIRST = (((0,), (0,)), ((), ()))
PLAIN = (((1,), (0,)), ((), ()))


def dot(a, b, dims=PLAIN, precision=None):
    return lax.dot_general(a, b, dims, precision=precision, preferred_element_type=jnp.float32)


def split_bf16(x):
    hi = x.astype(jnp.bfloat16)
    lo = (x - hi.astype(jnp.float32)).astype(jnp.bfloat16)
    return hi, lo


def dot3(a, b, dims=PLAIN):
    ah, al = split_bf16(a)
    bh, bl = split_bf16(b)
    return dot(ah, bh, dims) + (dot(ah, bl, dims) + dot(al, bh, dims))


def lanes(x):
    return jnp.broadcast_to(x, (8, LANES))


def factor_panel(s_ref, p_ref):
    sub_iota = lax.broadcasted_iota(jnp.int32, (8, LANES), 0)
    rows = [[s_ref[8 * g : 8 * g + 8, LANES * t : LANES * (t + 1)] for t in range(TW)] for g in range(G8)]
    for b in range(G8):
        c0 = 8 * b
        col = [[lanes(rows[g][0][:, c0 + j : c0 + j + 1]) for j in range(8)] for g in range(b, G8)]
        e = [[lanes(col[0][j][i : i + 1, :]) for j in range(i + 1)] for i in range(8)]
        r = []
        l = [[None] * 8 for _ in range(8)]
        for j in range(8):
            rj = lax.rsqrt(e[j][j])
            r.append(rj)
            for i in range(j + 1, 8):
                l[i][j] = e[i][j] * rj
            for i in range(j + 1, 8):
                for k in range(j + 1, i + 1):
                    e[i][k] = e[i][k] - l[i][j] * l[k][j]
        y = []
        for i in range(8):
            yi = []
            for t in range(TW):
                v = lanes(rows[b][t][i : i + 1, :])
                for j in range(i):
                    v = v - l[i][j] * y[j][t]
                yi.append(v * r[i])
            y.append(yi)
        for t in range(TW):
            u = y[0][t]
            for i in range(1, 8):
                u = jnp.where(sub_iota == i, y[i][t], u)
            p_ref[8 * b : 8 * b + 8, LANES * t : LANES * (t + 1)] = u
        for g in range(b + 1, G8):
            cs = []
            for j in range(8):
                v = col[g - b][j]
                for k in range(j):
                    v = v - l[j][k] * cs[k]
                cs.append(v * r[j])
            for t in range(TW):
                v = rows[g][t]
                for j in range(8):
                    v = v - cs[j] * y[j][t]
                rows[g][t] = v


def factor_kernel(d_ref, f_ref, z_ref, x_ref, a_ref, s_ref, p_ref, u_ref):
    row_i = lax.broadcasted_iota(jnp.int32, (B, B), 0)
    col_i = lax.broadcasted_iota(jnp.int32, (B, B), 1)
    a_ref[...] = d_ref[:B]

    def panel(turn, carry):
        s_ref[:, :B] = a_ref[...]
        s_ref[:, B:] = jnp.where(row_i == col_i, 1.0, 0.0)

        def step(k, carry):
            factor_panel(s_ref, p_ref)
            start = pl.multiple_of(k * SUB, SUB)
            u_ref[pl.ds(start, SUB), :] = pltpu.roll(p_ref[:, :B], start, 1)
            z_ref[turn, pl.ds(start, SUB), :] = p_ref[:, B:]
            left = p_ref[:, :B]
            rolled = pltpu.roll(left, B - SUB, 1)
            lane = lax.broadcasted_iota(jnp.int32, (SUB, B), 1)
            rolled = jnp.where(lane < B - SUB, rolled, 0.0)
            upd_a = dot(rolled, rolled, FIRST, HIGHEST)
            upd_z = dot(rolled, p_ref[:, B:], FIRST, HIGHEST)
            keep = B - SUB
            old = pltpu.roll(s_ref[SUB:, :B], B - SUB, 1)
            lane2 = lax.broadcasted_iota(jnp.int32, (keep, B), 1)
            old = jnp.where(lane2 < keep, old, 0.0)
            old_z = s_ref[SUB:, B:]
            s_ref[:keep, :B] = old - upd_a[:keep]
            s_ref[:keep, B:] = old_z - upd_z[:keep]
            s_ref[keep:, :] = jnp.zeros((SUB, 2 * B), jnp.float32)
            return carry

        lax.fori_loop(0, B // SUB, step, 0)

        z_ref[turn] = jnp.where(row_i >= col_i, z_ref[turn], 0.0)
        f_ref[turn] = jnp.where(row_i >= col_i, u_ref[...].T, 0.0)

        @pl.when(turn == 0)
        def _():
            low = dot3(d_ref[B : 2 * B], z_ref[0], LAST)
            half = low.astype(jnp.bfloat16)
            x_ref[...] = half
            a_ref[...] = d_ref[2 * B : 3 * B] - dot(half, half, LAST)

        return carry

    lax.fori_loop(0, PANELS, panel, 0)


def factor_pair(blocks):
    return pl.pallas_call(
        factor_kernel,
        out_shape=(
            jax.ShapeDtypeStruct((PANELS, B, B), jnp.float32),
            jax.ShapeDtypeStruct((PANELS, B, B), jnp.float32),
            jax.ShapeDtypeStruct((B, B), jnp.bfloat16),
        ),
        scratch_shapes=[
            pltpu.VMEM((B, B), jnp.float32),
            pltpu.VMEM((B, 2 * B), jnp.float32),
            pltpu.VMEM((SUB, 2 * B), jnp.float32),
            pltpu.VMEM((B, B), jnp.float32),
        ],
        cost_estimate=pl.CostEstimate(flops=100_000_000, bytes_accessed=2_000_000, transcendentals=0),
    )(blocks)


def tail_kernel(
    ro_ref, co_ref, at_ref, w_ref, cols_ref, rowp_ref, f_ref, z_ref, x_ref, vs_ref, v_ref,
    o_ref, vout_ref, q_ref, full_ref, half_ref, *, rb, cb,
):
    j = pl.program_id(0)
    g = at_ref[0]

    @pl.when(j == 0)
    def _():
        h, n = vs_ref.shape[0] // 2, v_ref.shape[0]
        x = x_ref[...]
        for k in range(cb):
            span = slice(k * B, (k + 1) * B)
            own = co_ref[k]
            q0 = dot3(z_ref[0], rowp_ref[:B, span].astype(jnp.float32))
            q0 = jnp.where(own > g, q0, 0.0).astype(jnp.bfloat16)
            r1 = rowp_ref[B:, span].astype(jnp.float32) - dot(x, q0)
            q1 = dot3(z_ref[1], r1)
            q_ref[:B, span] = q0
            q_ref[B:, span] = jnp.where(own > g + 1, q1, 0.0).astype(jnp.bfloat16)
        for i in range(rb):
            span = slice(i * B, (i + 1) * B)
            own = ro_ref[i]
            p0 = dot3(cols_ref[span, :B], z_ref[0], LAST)
            p0 = jnp.where(own > g, p0, 0.0)
            h0 = p0.astype(jnp.bfloat16)
            c1 = cols_ref[span, B:] - dot(h0, x, LAST)
            p1 = dot3(c1, z_ref[1], LAST)
            p1 = jnp.where(own > g + 1, p1, 0.0)
            full_ref[span, :B] = p0
            full_ref[span, B:] = p1
            half_ref[span, :B] = h0
            half_ref[span, B:] = p1.astype(jnp.bfloat16)
        w0 = dot(vs_ref[:h], z_ref[0], LAST, HIGHEST)
        w0h = w0.astype(jnp.bfloat16)
        w1 = dot(vs_ref[h:] - dot(w0h, x, LAST), z_ref[1], LAST, HIGHEST)
        w1h = w1.astype(jnp.bfloat16)
        for i in range(rb):
            span = slice(i * B, (i + 1) * B)
            own = ro_ref[i]
            new = v_ref[:, span] - (dot(w0h, half_ref[span, :B], LAST) + dot(w1h, half_ref[span, B:], LAST))
            new = jnp.where(own == g, w0, new)
            vout_ref[:, span] = jnp.where(own == g + 1, w1, new)

    cown = co_ref[j]
    start = pl.multiple_of(j * B, B)
    o_ref[...] = w_ref[...] - dot(half_ref[...], q_ref[:, pl.ds(start, B)])

    @pl.when(cown > g)
    def _():
        for i in range(rb):
            rown = ro_ref[i]

            @pl.when((rown == g) | ((rown == g + 1) & (cown > g + 1)))
            def _():
                o_ref[i * B : (i + 1) * B] = jnp.zeros((B, B), jnp.float32)

    for turn in range(PANELS):
        @pl.when(cown == g + turn)
        def _():
            for i in range(rb):
                span = slice(i * B, (i + 1) * B)
                rown = ro_ref[i]

                @pl.when(rown > g + turn)
                def _():
                    o_ref[span] = full_ref[span, turn * B : (turn + 1) * B]

                @pl.when(rown == g + turn)
                def _():
                    o_ref[span] = f_ref[turn]


def tail(ro, co, at, w, cols, rowp, factors, z, x, everyone, v):
    rows, width = w.shape
    fixed = lambda rank, *at: (lambda j, a, b, c: tuple(at) if at else (0,) * rank)
    stripe = lambda j, a, b, c: (0, j)
    heads = everyone.shape[0] - 3 * B
    whole = lambda x: pl.BlockSpec(x.shape, fixed(x.ndim))
    return pl.pallas_call(
        functools.partial(tail_kernel, rb=rows // B, cb=width // B),
        grid_spec=pltpu.PrefetchScalarGridSpec(
            num_scalar_prefetch=3,
            grid=(width // B,),
            in_specs=[
                pl.BlockSpec((rows, B), stripe),
                whole(cols),
                whole(rowp),
                whole(factors),
                whole(z),
                whole(x),
                pl.BlockSpec((heads, B), fixed(2, 3 * B // heads, 0)),
                whole(v),
            ],
            out_specs=[pl.BlockSpec((rows, B), stripe), whole(v)],
            scratch_shapes=[
                pltpu.VMEM((2 * B, width), jnp.bfloat16),
                pltpu.VMEM((rows, 2 * B), jnp.float32),
                pltpu.VMEM((rows, 2 * B), jnp.bfloat16),
            ],
        ),
        out_shape=(jax.ShapeDtypeStruct(w.shape, w.dtype), jax.ShapeDtypeStruct(v.shape, v.dtype)),
    )(ro, co, at, w, cols, rowp, factors, z, x, everyone, v)


def prep_kernel(at_ref, wc_ref, wr_ref, cols_ref, rowp_ref):
    t = pl.program_id(0)
    cols_ref[...] = jnp.where(at_ref[4 + t] > 0, wc_ref[...], 0.0)
    rowp_ref[...] = jnp.where(at_ref[6 + t] > 0, wr_ref[...], 0.0).astype(jnp.bfloat16)


def prep(at, w):
    rows, width = w.shape
    return pl.pallas_call(
        prep_kernel,
        grid_spec=pltpu.PrefetchScalarGridSpec(
            num_scalar_prefetch=1,
            grid=(PANELS,),
            in_specs=[
                pl.BlockSpec((rows, B), lambda t, a: (0, a[t])),
                pl.BlockSpec((B, width), lambda t, a: (a[2 + t], 0)),
            ],
            out_specs=[
                pl.BlockSpec((rows, B), lambda t, a: (0, t)),
                pl.BlockSpec((B, width), lambda t, a: (t, 0)),
            ],
        ),
        out_shape=(
            jax.ShapeDtypeStruct((rows, PANELS * B), jnp.float32),
            jax.ShapeDtypeStruct((PANELS * B, width), jnp.bfloat16),
        ),
    )(at, w, w)


MESH = pl.DeviceIdType.MESH
CHUNKS = 16


def remote(src, dst, send, recv, where):
    return pltpu.make_async_remote_copy(
        src_ref=src, dst_ref=dst, send_sem=send, recv_sem=recv, device_id=where, device_id_type=MESH
    )


class RowSpread:
    def __init__(self, axis_size, in_ref, acc_ref, core_ref, hop_ref, send, recv):
        self.bits = [1 << b for b in range(1, axis_size.bit_length() - 1)]
        self.in_ref, self.acc, self.core, self.hop = in_ref, acc_ref, core_ref, hop_ref
        self.send, self.recv = send, recv
        me = lax.axis_index("row")
        self.me = me
        self.odd = lax.rem(me, 2)
        self.mate = me + 1 - 2 * self.odd
        self.rows = in_ref.shape[0]
        self.half = self.rows // 2
        self.quarter = self.rows // 4
        self.stages = len(self.bits)

    def mine(self, part=0, size=None):
        start = self.odd * self.half + part * self.quarter
        return pl.ds(pl.multiple_of(start, self.quarter), self.half if size is None else size)

    def theirs(self):
        start = (1 - self.odd) * self.half
        return pl.ds(pl.multiple_of(start, self.half), self.half)

    def partner(self, bit):
        digit = lax.rem(self.me // bit, 2)
        return {"row": self.me + bit - 2 * bit * digit}

    def first(self):
        return remote(self.in_ref.at[self.theirs()], self.core, self.send.at[0], self.recv.at[0], {"row": self.mate})

    def middle(self, stage, part):
        bit = self.bits[(stage + part) % self.stages]
        index = 1 + 2 * stage + part
        return remote(
            self.acc.at[self.mine(part, self.quarter)],
            self.hop.at[stage, part],
            self.send.at[index],
            self.recv.at[index],
            self.partner(bit),
        )

    def final(self):
        index = 1 + 2 * self.stages
        rows = self.acc.at[self.mine()]
        return remote(rows, rows, self.send.at[index], self.recv.at[index], {"row": self.mate})

    def start(self):
        self.first().start()

    def advance(self, turn):
        if turn == 0:
            self.first().wait()
            self.acc[self.mine()] = self.in_ref[self.mine()] + self.core[...]
        else:
            for part in range(2):
                self.middle(turn - 1, part).wait()
                rows = self.mine(part, self.quarter)
                self.acc[rows] = self.acc[rows] + self.hop[turn - 1, part]
        if turn < self.stages:
            for part in range(2):
                self.middle(turn, part).start()
        else:
            self.final().start()

    def finish(self):
        self.final().wait()


def spread_scratch(axis_size, shape, dtype):
    stages = axis_size.bit_length() - 2
    rows, width = shape
    count = 2 + 2 * stages
    return [
        pltpu.VMEM((rows // 2, width), dtype),
        pltpu.VMEM((stages, 2, rows // 4, width), dtype),
        pltpu.SemaphoreType.DMA((count,)),
        pltpu.SemaphoreType.DMA((count,)),
    ]


def gather_kernel(
    nr, nc, own, rowp, inn, out, rowout, v,
    rin, lin, rtx, ltx, rs, rr, ls, lr,
    core, hop, rowsend, rowrecv, vsend, vrecv, vself,
):
    r = lax.axis_index("row")
    c = lax.axis_index("col")
    size = own.shape[0] // CHUNKS
    ratio = nr // nc
    spread = RowSpread(nr, rowp, rowout, core, hop, rowsend, rowrecv)
    part_p, width = inn.shape[1], inn.shape[2]

    def chunk(q):
        return pl.ds(pl.multiple_of(q * size, size), size)

    def right(src, q):
        return remote(src.at[chunk(q)], rin.at[chunk(q)], rs.at[q], rr.at[q], {"col": c + 1})

    def left(src, q):
        return remote(src.at[chunk(q)], lin.at[chunk(q)], ls.at[q], lr.at[q], {"col": c - 1})

    spread.start()

    @pl.when(c == 0)
    def _():
        lax.fori_loop(0, CHUNKS, lambda q, k: (right(own, q).start(), k)[1], 0)
        rin[...] = jnp.zeros_like(rin)

    @pl.when(c == nc - 1)
    def _():
        lax.fori_loop(0, CHUNKS, lambda q, k: (left(own, q).start(), k)[1], 0)
        lin[...] = jnp.zeros_like(lin)

    my_col = r // ratio

    def v_copy(group):
        place = v.at[
            pl.ds(pl.multiple_of(lax.rem(r, ratio) * part_p, part_p), part_p),
            pl.ds(pl.multiple_of(c * width, width), width),
        ]
        slot = lax.rem(r, ratio) * nc + c
        return remote(inn.at[group], place, vsend.at[group], vrecv.at[slot], {"row": group, "col": my_col})

    def v_local():
        place = v.at[
            pl.ds(pl.multiple_of(lax.rem(r, ratio) * part_p, part_p), part_p),
            pl.ds(pl.multiple_of(c * width, width), width),
        ]
        return pltpu.make_async_copy(inn.at[r], place, vself)

    for shift in range(nr):
        group = lax.rem(r + shift, nr)
        if shift == 0:
            @pl.when(my_col == c)
            def _():
                v_local().start()

            @pl.when(my_col != c)
            def _():
                v_copy(group).start()
        else:
            v_copy(group).start()

    steps = CHUNKS + nc - 2

    def relay(t, carry):
        q = t - (c - 1)

        @pl.when((c > 0) & (q >= 0) & (q < CHUNKS))
        def _():
            right(own, q).wait_recv()

            @pl.when(c < nc - 1)
            def _():
                rtx[chunk(q)] = rin[chunk(q)] + own[chunk(q)]
                right(rtx, q).start()

        p = t - (nc - 2 - c)

        @pl.when((c < nc - 1) & (p >= 0) & (p < CHUNKS))
        def _():
            left(own, p).wait_recv()

            @pl.when(c > 0)
            def _():
                ltx[chunk(p)] = lin[chunk(p)] + own[chunk(p)]
                left(ltx, p).start()

        return carry

    turns = spread.stages + 1
    begin = 0
    for turn in range(turns):
        end = 1 + (steps - 1) * (turn + 1) // (turns + 1)
        lax.fori_loop(begin, end, relay, 0)
        begin = end
        spread.advance(turn)
    lax.fori_loop(begin, steps, relay, 0)

    def total(q, carry):
        out[chunk(q)] = own[chunk(q)] + (rin[chunk(q)] + lin[chunk(q)])
        return carry

    lax.fori_loop(0, CHUNKS, total, 0)

    @pl.when(c < nc - 1)
    def _():
        lax.fori_loop(0, CHUNKS, lambda q, k: (right(own, q).wait_send(), k)[1], 0)

    @pl.when(c > 0)
    def _():
        lax.fori_loop(0, CHUNKS, lambda q, k: (left(own, q).wait_send(), k)[1], 0)

    spread.finish()
    for shift in range(nr):
        group = lax.rem(r + shift, nr)
        if shift == 0:
            @pl.when(my_col == c)
            def _():
                v_local().wait()

            @pl.when(my_col != c)
            def _():
                v_copy(group).wait_send()
        else:
            v_copy(group).wait_send()
    for a in range(ratio):
        for b in range(nc):
            @pl.when((r != ratio * c + a) | (c != b))
            def _():
                place = v.at[pl.ds(a * part_p, part_p), pl.ds(b * width, width)]
                remote(
                    inn.at[0], place, vsend.at[0], vrecv.at[a * nc + b], {"row": r, "col": c}
                ).wait_recv()


def gather(nr, nc, own, rowp, inn):
    rows, width = own.shape
    vmem = pl.BlockSpec(memory_space=pltpu.VMEM)
    ratio = nr // nc
    big = pltpu.VMEM((rows, width), jnp.float32)
    sems = pltpu.SemaphoreType.DMA((CHUNKS,))
    return pl.pallas_call(
        functools.partial(gather_kernel, nr, nc),
        out_shape=(
            jax.ShapeDtypeStruct(own.shape, own.dtype),
            jax.ShapeDtypeStruct(rowp.shape, rowp.dtype),
            jax.ShapeDtypeStruct((ratio * inn.shape[1], nc * inn.shape[2]), inn.dtype),
        ),
        in_specs=[vmem] * 3,
        out_specs=(vmem,) * 3,
        scratch_shapes=[big] * 4 + [sems] * 4
        + spread_scratch(nr, rowp.shape, rowp.dtype)
        + [
            pltpu.SemaphoreType.DMA((nr,)),
            pltpu.SemaphoreType.DMA((ratio * nc,)),
            pltpu.SemaphoreType.DMA,
        ],
        compiler_params=pltpu.CompilerParams(has_side_effects=True),
    )(own, rowp, inn)


def spread_kernel(nr, in_ref, out_ref, core, hop, send, recv):
    spread = RowSpread(nr, in_ref, out_ref, core, hop, send, recv)
    spread.start()
    for turn in range(spread.stages + 1):
        spread.advance(turn)
    spread.finish()


def spread_rows(nr, value):
    vmem = pl.BlockSpec(memory_space=pltpu.VMEM)
    return pl.pallas_call(
        functools.partial(spread_kernel, nr),
        out_shape=jax.ShapeDtypeStruct(value.shape, value.dtype),
        in_specs=[vmem],
        out_specs=vmem,
        scratch_shapes=spread_scratch(nr, value.shape, value.dtype),
        compiler_params=pltpu.CompilerParams(has_side_effects=True),
    )(value)


def locate(block_owner, target):
    positions = jnp.arange(block_owner.shape[0], dtype=jnp.int32)
    return jnp.sum(jnp.where(block_owner == target, positions, 0))


def per_device(covariance, innovations, block_owner, panel_index):
    local_rows, local_cols = covariance.shape
    row_blocks = local_rows // B
    column_blocks = local_cols // B
    r_here = lax.axis_index("row")
    c_here = lax.axis_index("col")
    nr, nc = lax.axis_size("row"), lax.axis_size("col")
    g = panel_index[0]
    slots = [locate(block_owner, g + t) for t in range(PANELS)]
    rroot = [s // row_blocks for s in slots]
    croot = [s // column_blocks for s in slots]
    rstart = [s % row_blocks * B for s in slots]
    places = jnp.stack(
        [s % column_blocks for s in slots]
        + [s % row_blocks for s in slots]
        + [(c_here == c).astype(jnp.int32) for c in croot]
        + [(r_here == r).astype(jnp.int32) for r in rroot]
    ).astype(jnp.int32)
    cols, rowpanel = prep(places, covariance)
    cols, rowpanel, v = gather(nr, nc, cols, rowpanel, innovations.transpose(1, 0, 2))

    def pick(value, t, axis):
        tile = lax.dynamic_slice_in_dim(value, rstart[t], B, axis)
        return jnp.where(r_here == rroot[t], tile, 0.0)

    parts = [pick(cols[:, :B], 0, 0), pick(cols[:, :B], 1, 0), pick(cols[:, B:], 1, 0), pick(v, 0, 1), pick(v, 1, 1)]
    everyone = spread_rows(nr, jnp.concatenate(parts, axis=0))
    factors, z, x = factor_pair(everyone)
    ro = lax.dynamic_slice_in_dim(block_owner, r_here * row_blocks, row_blocks)
    co = lax.dynamic_slice_in_dim(block_owner, c_here * column_blocks, column_blocks)
    return tail(ro, co, panel_index, covariance, cols, rowpanel, factors, z, x, everyone, v)


def solution(mesh):
    placed = (P("row", "col"), P("row", None, "col"), P(), P())
    return jax.shard_map(
        per_device,
        mesh=mesh,
        in_specs=placed,
        out_specs=(P("row", "col"), P("col", "row")),
        check_vma=False,
    )
```

```python
import functools

import jax
import jax.numpy as jnp
from jax import lax
from jax.experimental import pallas as pl
from jax.experimental.pallas import tpu as pltpu
from jax.sharding import PartitionSpec as P

B = 256
PANELS = 2
SUB = 64
G8 = SUB // 8
LANES = 128
TW = 2 * B // LANES
HIGHEST = lax.Precision.HIGHEST

LAST = (((1,), (1,)), ((), ()))
FIRST = (((0,), (0,)), ((), ()))
PLAIN = (((1,), (0,)), ((), ()))


def dot(a, b, dims=PLAIN, precision=None):
    return lax.dot_general(a, b, dims, precision=precision, preferred_element_type=jnp.float32)


def split_bf16(x):
    hi = x.astype(jnp.bfloat16)
    lo = (x - hi.astype(jnp.float32)).astype(jnp.bfloat16)
    return hi, lo


def dot3(a, b, dims=PLAIN):
    ah, al = split_bf16(a)
    bh, bl = split_bf16(b)
    return dot(ah, bh, dims) + (dot(ah, bl, dims) + dot(al, bh, dims))


def lanes(x):
    return jnp.broadcast_to(x, (8, LANES))


def factor_panel(s_ref, p_ref):
    sub_iota = lax.broadcasted_iota(jnp.int32, (8, LANES), 0)
    rows = [[s_ref[8 * g : 8 * g + 8, LANES * t : LANES * (t + 1)] for t in range(TW)] for g in range(G8)]
    for b in range(G8):
        c0 = 8 * b
        col = [[lanes(rows[g][0][:, c0 + j : c0 + j + 1]) for j in range(8)] for g in range(b, G8)]
        e = [[lanes(col[0][j][i : i + 1, :]) for j in range(i + 1)] for i in range(8)]
        r = []
        l = [[None] * 8 for _ in range(8)]
        for j in range(8):
            rj = lax.rsqrt(e[j][j])
            r.append(rj)
            for i in range(j + 1, 8):
                l[i][j] = e[i][j] * rj
            for i in range(j + 1, 8):
                for k in range(j + 1, i + 1):
                    e[i][k] = e[i][k] - l[i][j] * l[k][j]
        y = []
        for i in range(8):
            yi = []
            for t in range(TW):
                v = lanes(rows[b][t][i : i + 1, :])
                for j in range(i):
                    v = v - l[i][j] * y[j][t]
                yi.append(v * r[i])
            y.append(yi)
        for t in range(TW):
            u = y[0][t]
            for i in range(1, 8):
                u = jnp.where(sub_iota == i, y[i][t], u)
            p_ref[8 * b : 8 * b + 8, LANES * t : LANES * (t + 1)] = u
        for g in range(b + 1, G8):
            cs = []
            for j in range(8):
                v = col[g - b][j]
                for k in range(j):
                    v = v - l[j][k] * cs[k]
                cs.append(v * r[j])
            for t in range(TW):
                v = rows[g][t]
                for j in range(8):
                    v = v - cs[j] * y[j][t]
                rows[g][t] = v


def factor_kernel(d_ref, f_ref, z_ref, x_ref, a_ref, s_ref, p_ref, u_ref):
    row_i = lax.broadcasted_iota(jnp.int32, (B, B), 0)
    col_i = lax.broadcasted_iota(jnp.int32, (B, B), 1)
    a_ref[...] = d_ref[:B]

    def panel(turn, carry):
        s_ref[:, :B] = a_ref[...]
        s_ref[:, B:] = jnp.where(row_i == col_i, 1.0, 0.0)

        def step(k, carry):
            factor_panel(s_ref, p_ref)
            start = pl.multiple_of(k * SUB, SUB)
            u_ref[pl.ds(start, SUB), :] = pltpu.roll(p_ref[:, :B], start, 1)
            z_ref[turn, pl.ds(start, SUB), :] = p_ref[:, B:]
            left = p_ref[:, :B]
            rolled = pltpu.roll(left, B - SUB, 1)
            lane = lax.broadcasted_iota(jnp.int32, (SUB, B), 1)
            rolled = jnp.where(lane < B - SUB, rolled, 0.0)
            upd_a = dot(rolled, rolled, FIRST, HIGHEST)
            upd_z = dot(rolled, p_ref[:, B:], FIRST, HIGHEST)
            keep = B - SUB
            old = pltpu.roll(s_ref[SUB:, :B], B - SUB, 1)
            lane2 = lax.broadcasted_iota(jnp.int32, (keep, B), 1)
            old = jnp.where(lane2 < keep, old, 0.0)
            old_z = s_ref[SUB:, B:]
            s_ref[:keep, :B] = old - upd_a[:keep]
            s_ref[:keep, B:] = old_z - upd_z[:keep]
            s_ref[keep:, :] = jnp.zeros((SUB, 2 * B), jnp.float32)
            return carry

        lax.fori_loop(0, B // SUB, step, 0)

        z_ref[turn] = jnp.where(row_i >= col_i, z_ref[turn], 0.0)
        f_ref[turn] = jnp.where(row_i >= col_i, u_ref[...].T, 0.0)

        @pl.when(turn == 0)
        def _():
            low = dot3(d_ref[B : 2 * B], z_ref[0], LAST)
            half = low.astype(jnp.bfloat16)
            x_ref[...] = half
            a_ref[...] = d_ref[2 * B : 3 * B] - dot(half, half, LAST)

        return carry

    lax.fori_loop(0, PANELS, panel, 0)


def factor_pair(blocks):
    return pl.pallas_call(
        factor_kernel,
        out_shape=(
            jax.ShapeDtypeStruct((PANELS, B, B), jnp.float32),
            jax.ShapeDtypeStruct((PANELS, B, B), jnp.float32),
            jax.ShapeDtypeStruct((B, B), jnp.bfloat16),
        ),
        scratch_shapes=[
            pltpu.VMEM((B, B), jnp.float32),
            pltpu.VMEM((B, 2 * B), jnp.float32),
            pltpu.VMEM((SUB, 2 * B), jnp.float32),
            pltpu.VMEM((B, B), jnp.float32),
        ],
        cost_estimate=pl.CostEstimate(flops=100_000_000, bytes_accessed=2_000_000, transcendentals=0),
    )(blocks)


def tail_kernel(
    own_ref, at_ref, w_ref, cols_ref, rowp_ref, f_ref, z_ref, x_ref, vs_ref, v_ref,
    o_ref, vout_ref, q_ref, full_ref, half_ref, *, rb, cb,
):
    j = pl.program_id(0)
    g = at_ref[0]

    @pl.when(j == 0)
    def _():
        h, n = vs_ref.shape[0] // 2, v_ref.shape[0]
        x = x_ref[...]
        for k in range(cb):
            span = slice(k * B, (k + 1) * B)
            own = own_ref[at_ref[2] + k]
            q0 = dot3(z_ref[0], rowp_ref[:B, span].astype(jnp.float32))
            q0 = jnp.where(own > g, q0, 0.0).astype(jnp.bfloat16)
            r1 = rowp_ref[B:, span].astype(jnp.float32) - dot(x, q0)
            q1 = dot3(z_ref[1], r1)
            q_ref[:B, span] = q0
            q_ref[B:, span] = jnp.where(own > g + 1, q1, 0.0).astype(jnp.bfloat16)
        for i in range(rb):
            span = slice(i * B, (i + 1) * B)
            own = own_ref[at_ref[1] + i]
            p0 = dot3(cols_ref[span, :B], z_ref[0], LAST)
            p0 = jnp.where(own > g, p0, 0.0)
            h0 = p0.astype(jnp.bfloat16)
            c1 = cols_ref[span, B:] - dot(h0, x, LAST)
            p1 = dot3(c1, z_ref[1], LAST)
            p1 = jnp.where(own > g + 1, p1, 0.0)
            full_ref[span, :B] = p0
            full_ref[span, B:] = p1
            half_ref[span, :B] = h0
            half_ref[span, B:] = p1.astype(jnp.bfloat16)
        w0 = dot(vs_ref[:h], z_ref[0], LAST, HIGHEST)
        w0h = w0.astype(jnp.bfloat16)
        w1 = dot(vs_ref[h:] - dot(w0h, x, LAST), z_ref[1], LAST, HIGHEST)
        w1h = w1.astype(jnp.bfloat16)
        for i in range(rb):
            span = slice(i * B, (i + 1) * B)
            own = own_ref[at_ref[1] + i]
            new = v_ref[:, span] - (dot(w0h, half_ref[span, :B], LAST) + dot(w1h, half_ref[span, B:], LAST))
            new = jnp.where(own == g, w0, new)
            vout_ref[:, span] = jnp.where(own == g + 1, w1, new)

    cown = own_ref[at_ref[2] + j]
    start = pl.multiple_of(j * B, B)
    o_ref[...] = w_ref[...] - dot(half_ref[...], q_ref[:, pl.ds(start, B)])

    @pl.when(cown > g)
    def _():
        for i in range(rb):
            rown = own_ref[at_ref[1] + i]

            @pl.when((rown == g) | ((rown == g + 1) & (cown > g + 1)))
            def _():
                o_ref[i * B : (i + 1) * B] = jnp.zeros((B, B), jnp.float32)

    for turn in range(PANELS):
        @pl.when(cown == g + turn)
        def _():
            for i in range(rb):
                span = slice(i * B, (i + 1) * B)
                rown = own_ref[at_ref[1] + i]

                @pl.when(rown > g + turn)
                def _():
                    o_ref[span] = full_ref[span, turn * B : (turn + 1) * B]

                @pl.when(rown == g + turn)
                def _():
                    o_ref[span] = f_ref[turn]


def tail(owner, at, w, cols, rowp, factors, z, x, everyone, v):
    rows, width = w.shape
    fixed = lambda rank, *at: (lambda j, a, b: tuple(at) if at else (0,) * rank)
    stripe = lambda j, a, b: (0, j)
    heads = everyone.shape[0] - 3 * B
    whole = lambda x: pl.BlockSpec(x.shape, fixed(x.ndim))
    return pl.pallas_call(
        functools.partial(tail_kernel, rb=rows // B, cb=width // B),
        grid_spec=pltpu.PrefetchScalarGridSpec(
            num_scalar_prefetch=2,
            grid=(width // B,),
            in_specs=[
                pl.BlockSpec((rows, B), stripe),
                whole(cols),
                whole(rowp),
                whole(factors),
                whole(z),
                whole(x),
                pl.BlockSpec((heads, B), fixed(2, 3 * B // heads, 0)),
                whole(v),
            ],
            out_specs=[pl.BlockSpec((rows, B), stripe), whole(v)],
            scratch_shapes=[
                pltpu.VMEM((2 * B, width), jnp.bfloat16),
                pltpu.VMEM((rows, 2 * B), jnp.float32),
                pltpu.VMEM((rows, 2 * B), jnp.bfloat16),
            ],
        ),
        out_shape=(jax.ShapeDtypeStruct(w.shape, w.dtype), jax.ShapeDtypeStruct(v.shape, v.dtype)),
    )(owner, at, w, cols, rowp, factors, z, x, everyone, v)


def prep_kernel(at_ref, wc_ref, wr_ref, cols_ref, rowp_ref):
    t = pl.program_id(0)
    cols_ref[...] = jnp.where(at_ref[4 + t] > 0, wc_ref[...], 0.0)
    rowp_ref[...] = jnp.where(at_ref[6 + t] > 0, wr_ref[...], 0.0).astype(jnp.bfloat16)


def prep(at, w):
    rows, width = w.shape
    return pl.pallas_call(
        prep_kernel,
        grid_spec=pltpu.PrefetchScalarGridSpec(
            num_scalar_prefetch=1,
            grid=(PANELS,),
            in_specs=[
                pl.BlockSpec((rows, B), lambda t, a: (0, a[t])),
                pl.BlockSpec((B, width), lambda t, a: (a[2 + t], 0)),
            ],
            out_specs=[
                pl.BlockSpec((rows, B), lambda t, a: (0, t)),
                pl.BlockSpec((B, width), lambda t, a: (t, 0)),
            ],
        ),
        out_shape=(
            jax.ShapeDtypeStruct((rows, PANELS * B), jnp.float32),
            jax.ShapeDtypeStruct((PANELS * B, width), jnp.bfloat16),
        ),
    )(at, w, w)


MESH = pl.DeviceIdType.MESH
CHUNKS = 32
LAG = 5


def remote(src, dst, send, recv, where):
    return pltpu.make_async_remote_copy(
        src_ref=src, dst_ref=dst, send_sem=send, recv_sem=recv, device_id=where, device_id_type=MESH
    )


class RowSpread:
    def __init__(self, axis_size, in_ref, acc_ref, core_ref, hop_ref, send, recv):
        self.bits = [1 << b for b in range(1, axis_size.bit_length() - 1)]
        self.in_ref, self.acc, self.core, self.hop = in_ref, acc_ref, core_ref, hop_ref
        self.send, self.recv = send, recv
        me = lax.axis_index("row")
        self.me = me
        self.odd = lax.rem(me, 2)
        self.mate = me + 1 - 2 * self.odd
        self.rows = in_ref.shape[0]
        self.half = self.rows // 2
        self.quarter = self.rows // 4
        self.stages = len(self.bits)

    def mine(self, part=0, size=None):
        start = self.odd * self.half + part * self.quarter
        return pl.ds(pl.multiple_of(start, self.quarter), self.half if size is None else size)

    def theirs(self):
        start = (1 - self.odd) * self.half
        return pl.ds(pl.multiple_of(start, self.half), self.half)

    def partner(self, bit):
        digit = lax.rem(self.me // bit, 2)
        return {"row": self.me + bit - 2 * bit * digit}

    def first(self):
        return remote(self.in_ref.at[self.theirs()], self.core, self.send.at[0], self.recv.at[0], {"row": self.mate})

    def middle(self, stage, part):
        bit = self.bits[(stage + part) % self.stages]
        index = 1 + 2 * stage + part
        return remote(
            self.acc.at[self.mine(part, self.quarter)],
            self.hop.at[stage, part],
            self.send.at[index],
            self.recv.at[index],
            self.partner(bit),
        )

    def final(self):
        index = 1 + 2 * self.stages
        rows = self.acc.at[self.mine()]
        return remote(rows, rows, self.send.at[index], self.recv.at[index], {"row": self.mate})

    def start(self):
        self.first().start()

    def advance(self, turn):
        if turn == 0:
            self.first().wait()
            self.acc[self.mine()] = self.in_ref[self.mine()] + self.core[...]
        else:
            for part in range(2):
                self.middle(turn - 1, part).wait()
                rows = self.mine(part, self.quarter)
                self.acc[rows] = self.acc[rows] + self.hop[turn - 1, part]
        if turn < self.stages:
            for part in range(2):
                self.middle(turn, part).start()
        else:
            self.final().start()

    def finish(self):
        self.final().wait()


def spread_scratch(axis_size, shape, dtype):
    stages = axis_size.bit_length() - 2
    rows, width = shape
    count = 2 + 2 * stages
    return [
        pltpu.VMEM((rows // 2, width), dtype),
        pltpu.VMEM((stages, 2, rows // 4, width), dtype),
        pltpu.SemaphoreType.DMA((count,)),
        pltpu.SemaphoreType.DMA((count,)),
    ]


def gather_kernel(
    nr, nc, own, rowp, inn, out, rowout, v,
    rin, lin, rtx, ltx, rs, rr, ls, lr,
    core, hop, rowsend, rowrecv, vsend, vrecv, vself,
):
    r = lax.axis_index("row")
    c = lax.axis_index("col")
    size = own.shape[0] // CHUNKS
    ratio = nr // nc
    spread = RowSpread(nr, rowp, rowout, core, hop, rowsend, rowrecv)
    part_p, width = inn.shape[1], inn.shape[2]

    def chunk(q):
        return pl.ds(pl.multiple_of(q * size, size), size)

    def right(src, q):
        return remote(src.at[chunk(q)], rin.at[chunk(q)], rs.at[q], rr.at[q], {"col": c + 1})

    def left(src, q):
        return remote(src.at[chunk(q)], lin.at[chunk(q)], ls.at[q], lr.at[q], {"col": c - 1})

    spread.start()

    @pl.when(c == 0)
    def _():
        lax.fori_loop(0, CHUNKS, lambda q, k: (right(own, q).start(), k)[1], 0)
        rin[...] = jnp.zeros_like(rin)

    @pl.when(c == nc - 1)
    def _():
        lax.fori_loop(0, CHUNKS, lambda q, k: (left(own, q).start(), k)[1], 0)
        lin[...] = jnp.zeros_like(lin)

    my_col = r // ratio

    def v_copy(group):
        place = v.at[
            pl.ds(pl.multiple_of(lax.rem(r, ratio) * part_p, part_p), part_p),
            pl.ds(pl.multiple_of(c * width, width), width),
        ]
        slot = lax.rem(r, ratio) * nc + c
        return remote(inn.at[group], place, vsend.at[group], vrecv.at[slot], {"row": group, "col": my_col})

    def v_local():
        place = v.at[
            pl.ds(pl.multiple_of(lax.rem(r, ratio) * part_p, part_p), part_p),
            pl.ds(pl.multiple_of(c * width, width), width),
        ]
        return pltpu.make_async_copy(inn.at[r], place, vself)

    for shift in range(nr):
        group = lax.rem(r + shift, nr)
        if shift == 0:
            @pl.when(my_col == c)
            def _():
                v_local().start()

            @pl.when(my_col != c)
            def _():
                v_copy(group).start()
        else:
            v_copy(group).start()

    steps = CHUNKS + LAG * (nc - 2)

    def relay(t, carry):
        q = t - LAG * (c - 1)

        @pl.when((c > 0) & (q >= 0) & (q < CHUNKS))
        def _():
            right(own, q).wait_recv()

            @pl.when(c < nc - 1)
            def _():
                rtx[chunk(q)] = rin[chunk(q)] + own[chunk(q)]
                right(rtx, q).start()

        p = t - LAG * (nc - 2 - c)

        @pl.when((c < nc - 1) & (p >= 0) & (p < CHUNKS))
        def _():
            left(own, p).wait_recv()

            @pl.when(c > 0)
            def _():
                ltx[chunk(p)] = lin[chunk(p)] + own[chunk(p)]
                left(ltx, p).start()

        return carry

    turns = spread.stages + 1
    begin = 0
    for turn in range(turns):
        end = 1 + (steps - 1) * (turn + 1) // (turns + 1)
        lax.fori_loop(begin, end, relay, 0)
        begin = end
        spread.advance(turn)
    lax.fori_loop(begin, steps, relay, 0)

    def total(q, carry):
        out[chunk(q)] = own[chunk(q)] + (rin[chunk(q)] + lin[chunk(q)])
        return carry

    lax.fori_loop(0, CHUNKS, total, 0)

    @pl.when(c < nc - 1)
    def _():
        lax.fori_loop(0, CHUNKS, lambda q, k: (right(own, q).wait_send(), k)[1], 0)

    @pl.when(c > 0)
    def _():
        lax.fori_loop(0, CHUNKS, lambda q, k: (left(own, q).wait_send(), k)[1], 0)

    spread.finish()
    for shift in range(nr):
        group = lax.rem(r + shift, nr)
        if shift == 0:
            @pl.when(my_col == c)
            def _():
                v_local().wait()

            @pl.when(my_col != c)
            def _():
                v_copy(group).wait_send()
        else:
            v_copy(group).wait_send()
    for a in range(ratio):
        for b in range(nc):
            @pl.when((r != ratio * c + a) | (c != b))
            def _():
                place = v.at[pl.ds(a * part_p, part_p), pl.ds(b * width, width)]
                remote(
                    inn.at[0], place, vsend.at[0], vrecv.at[a * nc + b], {"row": r, "col": c}
                ).wait_recv()


def gather(nr, nc, own, rowp, inn):
    rows, width = own.shape
    vmem = pl.BlockSpec(memory_space=pltpu.VMEM)
    ratio = nr // nc
    big = pltpu.VMEM((rows, width), jnp.float32)
    sems = pltpu.SemaphoreType.DMA((CHUNKS,))
    return pl.pallas_call(
        functools.partial(gather_kernel, nr, nc),
        out_shape=(
            jax.ShapeDtypeStruct(own.shape, own.dtype),
            jax.ShapeDtypeStruct(rowp.shape, rowp.dtype),
            jax.ShapeDtypeStruct((ratio * inn.shape[1], nc * inn.shape[2]), inn.dtype),
        ),
        in_specs=[vmem] * 3,
        out_specs=(vmem,) * 3,
        scratch_shapes=[big] * 4 + [sems] * 4
        + spread_scratch(nr, rowp.shape, rowp.dtype)
        + [
            pltpu.SemaphoreType.DMA((nr,)),
            pltpu.SemaphoreType.DMA((ratio * nc,)),
            pltpu.SemaphoreType.DMA,
        ],
        compiler_params=pltpu.CompilerParams(has_side_effects=True),
    )(own, rowp, inn)


def spread_kernel(nr, in_ref, out_ref, core, hop, send, recv):
    spread = RowSpread(nr, in_ref, out_ref, core, hop, send, recv)
    spread.start()
    for turn in range(spread.stages + 1):
        spread.advance(turn)
    spread.finish()


def spread_rows(nr, value):
    vmem = pl.BlockSpec(memory_space=pltpu.VMEM)
    return pl.pallas_call(
        functools.partial(spread_kernel, nr),
        out_shape=jax.ShapeDtypeStruct(value.shape, value.dtype),
        in_specs=[vmem],
        out_specs=vmem,
        scratch_shapes=spread_scratch(nr, value.shape, value.dtype),
        compiler_params=pltpu.CompilerParams(has_side_effects=True),
    )(value)


def locate(block_owner, target):
    positions = jnp.arange(block_owner.shape[0], dtype=jnp.int32)
    return jnp.sum(jnp.where(block_owner == target, positions, 0))


def per_device(covariance, innovations, block_owner, panel_index):
    local_rows, local_cols = covariance.shape
    row_blocks = local_rows // B
    column_blocks = local_cols // B
    r_here = lax.axis_index("row")
    c_here = lax.axis_index("col")
    nr, nc = lax.axis_size("row"), lax.axis_size("col")
    g = panel_index[0]
    slots = [locate(block_owner, g + t) for t in range(PANELS)]
    rroot = [s // row_blocks for s in slots]
    croot = [s // column_blocks for s in slots]
    rstart = [s % row_blocks * B for s in slots]
    places = jnp.stack(
        [s % column_blocks for s in slots]
        + [s % row_blocks for s in slots]
        + [(c_here == c).astype(jnp.int32) for c in croot]
        + [(r_here == r).astype(jnp.int32) for r in rroot]
    ).astype(jnp.int32)
    cols, rowpanel = prep(places, covariance)
    cols, rowpanel, v = gather(nr, nc, cols, rowpanel, innovations.transpose(1, 0, 2))

    def pick(value, t, axis):
        tile = lax.dynamic_slice_in_dim(value, rstart[t], B, axis)
        return jnp.where(r_here == rroot[t], tile, 0.0)

    parts = [pick(cols[:, :B], 0, 0), pick(cols[:, :B], 1, 0), pick(cols[:, B:], 1, 0), pick(v, 0, 1), pick(v, 1, 1)]
    everyone = spread_rows(nr, jnp.concatenate(parts, axis=0))
    factors, z, x = factor_pair(everyone)
    at = jnp.stack([g, r_here * row_blocks, c_here * column_blocks]).astype(jnp.int32)
    return tail(block_owner, at, covariance, cols, rowpanel, factors, z, x, everyone, v)


def solution(mesh):
    placed = (P("row", "col"), P("row", None, "col"), P(), P())
    return jax.shard_map(
        per_device,
        mesh=mesh,
        in_specs=placed,
        out_specs=(P("row", "col"), P("col", "row")),
        check_vma=False,
    )
```

```python
import functools

import jax
import jax.numpy as jnp
from jax import lax
from jax.experimental import pallas as pl
from jax.experimental.pallas import tpu as pltpu
from jax.sharding import PartitionSpec as P

B = 256
PANELS = 2
SUB = 64
G8 = SUB // 8
LANES = 128
TW = 2 * B // LANES
HIGHEST = lax.Precision.HIGHEST

LAST = (((1,), (1,)), ((), ()))
FIRST = (((0,), (0,)), ((), ()))
PLAIN = (((1,), (0,)), ((), ()))


def dot(a, b, dims=PLAIN, precision=None):
    return lax.dot_general(a, b, dims, precision=precision, preferred_element_type=jnp.float32)


def split_bf16(x):
    hi = x.astype(jnp.bfloat16)
    lo = (x - hi.astype(jnp.float32)).astype(jnp.bfloat16)
    return hi, lo


def dot3(a, b, dims=PLAIN):
    ah, al = split_bf16(a)
    bh, bl = split_bf16(b)
    return dot(ah, bh, dims) + (dot(ah, bl, dims) + dot(al, bh, dims))


def lanes(x):
    return jnp.broadcast_to(x, (8, LANES))


def factor_panel(s_ref, p_ref):
    sub_iota = lax.broadcasted_iota(jnp.int32, (8, LANES), 0)
    rows = [[s_ref[8 * g : 8 * g + 8, LANES * t : LANES * (t + 1)] for t in range(TW)] for g in range(G8)]
    for b in range(G8):
        c0 = 8 * b
        col = [[lanes(rows[g][0][:, c0 + j : c0 + j + 1]) for j in range(8)] for g in range(b, G8)]
        e = [[lanes(col[0][j][i : i + 1, :]) for j in range(i + 1)] for i in range(8)]
        r = []
        l = [[None] * 8 for _ in range(8)]
        for j in range(8):
            rj = lax.rsqrt(e[j][j])
            r.append(rj)
            for i in range(j + 1, 8):
                l[i][j] = e[i][j] * rj
            for i in range(j + 1, 8):
                for k in range(j + 1, i + 1):
                    e[i][k] = e[i][k] - l[i][j] * l[k][j]
        y = []
        for i in range(8):
            yi = []
            for t in range(TW):
                v = lanes(rows[b][t][i : i + 1, :])
                for j in range(i):
                    v = v - l[i][j] * y[j][t]
                yi.append(v * r[i])
            y.append(yi)
        for t in range(TW):
            u = y[0][t]
            for i in range(1, 8):
                u = jnp.where(sub_iota == i, y[i][t], u)
            p_ref[8 * b : 8 * b + 8, LANES * t : LANES * (t + 1)] = u
        for g in range(b + 1, G8):
            cs = []
            for j in range(8):
                v = col[g - b][j]
                for k in range(j):
                    v = v - l[j][k] * cs[k]
                cs.append(v * r[j])
            for t in range(TW):
                v = rows[g][t]
                for j in range(8):
                    v = v - cs[j] * y[j][t]
                rows[g][t] = v


def factor_kernel(d_ref, f_ref, z_ref, x_ref, a_ref, s_ref, p_ref, u_ref):
    row_i = lax.broadcasted_iota(jnp.int32, (B, B), 0)
    col_i = lax.broadcasted_iota(jnp.int32, (B, B), 1)
    a_ref[...] = d_ref[:B]

    def panel(turn, carry):
        s_ref[:, :B] = a_ref[...]
        s_ref[:, B:] = jnp.where(row_i == col_i, 1.0, 0.0)

        def step(k, carry):
            factor_panel(s_ref, p_ref)
            start = pl.multiple_of(k * SUB, SUB)
            u_ref[pl.ds(start, SUB), :] = pltpu.roll(p_ref[:, :B], start, 1)
            z_ref[turn, pl.ds(start, SUB), :] = p_ref[:, B:]
            left = p_ref[:, :B]
            rolled = pltpu.roll(left, B - SUB, 1)
            lane = lax.broadcasted_iota(jnp.int32, (SUB, B), 1)
            rolled = jnp.where(lane < B - SUB, rolled, 0.0)
            upd_a = dot(rolled, rolled, FIRST, HIGHEST)
            upd_z = dot(rolled, p_ref[:, B:], FIRST, HIGHEST)
            keep = B - SUB
            old = pltpu.roll(s_ref[SUB:, :B], B - SUB, 1)
            lane2 = lax.broadcasted_iota(jnp.int32, (keep, B), 1)
            old = jnp.where(lane2 < keep, old, 0.0)
            old_z = s_ref[SUB:, B:]
            s_ref[:keep, :B] = old - upd_a[:keep]
            s_ref[:keep, B:] = old_z - upd_z[:keep]
            s_ref[keep:, :] = jnp.zeros((SUB, 2 * B), jnp.float32)
            return carry

        lax.fori_loop(0, B // SUB, step, 0)

        z_ref[turn] = jnp.where(row_i >= col_i, z_ref[turn], 0.0)
        f_ref[turn] = jnp.where(row_i >= col_i, u_ref[...].T, 0.0)

        @pl.when(turn == 0)
        def _():
            low = dot3(d_ref[B : 2 * B], z_ref[0], LAST)
            half = low.astype(jnp.bfloat16)
            x_ref[...] = half
            a_ref[...] = d_ref[2 * B : 3 * B] - dot(half, half, LAST)

        return carry

    lax.fori_loop(0, PANELS, panel, 0)


def factor_pair(blocks):
    return pl.pallas_call(
        factor_kernel,
        out_shape=(
            jax.ShapeDtypeStruct((PANELS, B, B), jnp.float32),
            jax.ShapeDtypeStruct((PANELS, B, B), jnp.float32),
            jax.ShapeDtypeStruct((B, B), jnp.bfloat16),
        ),
        scratch_shapes=[
            pltpu.VMEM((B, B), jnp.float32),
            pltpu.VMEM((B, 2 * B), jnp.float32),
            pltpu.VMEM((SUB, 2 * B), jnp.float32),
            pltpu.VMEM((B, B), jnp.float32),
        ],
        cost_estimate=pl.CostEstimate(flops=100_000_000, bytes_accessed=2_000_000, transcendentals=0),
    )(blocks)


def tail_kernel(
    own_ref, at_ref, w_ref, cols_ref, rowp_ref, f_ref, z_ref, x_ref, vs_ref, v_ref,
    o_ref, vout_ref, q_ref, full_ref, half_ref, *, rb, cb,
):
    j = pl.program_id(0)
    g = at_ref[8]

    @pl.when(j == 0)
    def _():
        h, n = vs_ref.shape[0] // 2, v_ref.shape[0]
        x = x_ref[...]
        for k in range(cb):
            span = slice(k * B, (k + 1) * B)
            own = own_ref[at_ref[10] + k]
            zh, zl = split_bf16(z_ref[0])
            q0 = dot(zh, rowp_ref[:B, span]) + dot(zl, rowp_ref[:B, span])
            q0 = jnp.where(own > g, q0, 0.0).astype(jnp.bfloat16)
            r1 = rowp_ref[B:, span].astype(jnp.float32) - dot(x, q0)
            q1 = dot3(z_ref[1], r1)
            q_ref[:B, span] = q0
            q_ref[B:, span] = jnp.where(own > g + 1, q1, 0.0).astype(jnp.bfloat16)
        for i in range(rb):
            span = slice(i * B, (i + 1) * B)
            own = own_ref[at_ref[9] + i]
            p0 = dot3(cols_ref[span, :B], z_ref[0], LAST)
            p0 = jnp.where(own > g, p0, 0.0)
            h0 = p0.astype(jnp.bfloat16)
            c1 = cols_ref[span, B:] - dot(h0, x, LAST)
            p1 = dot3(c1, z_ref[1], LAST)
            p1 = jnp.where(own > g + 1, p1, 0.0)
            full_ref[span, :B] = p0
            full_ref[span, B:] = p1
            half_ref[span, :B] = h0
            half_ref[span, B:] = p1.astype(jnp.bfloat16)
        w0 = dot(vs_ref[:h], z_ref[0], LAST, HIGHEST)
        w0h = w0.astype(jnp.bfloat16)
        w1 = dot(vs_ref[h:] - dot(w0h, x, LAST), z_ref[1], LAST, HIGHEST)
        w1h = w1.astype(jnp.bfloat16)
        for i in range(rb):
            span = slice(i * B, (i + 1) * B)
            own = own_ref[at_ref[9] + i]
            new = v_ref[:, span] - (dot(w0h, half_ref[span, :B], LAST) + dot(w1h, half_ref[span, B:], LAST))
            new = jnp.where(own == g, w0, new)
            vout_ref[:, span] = jnp.where(own == g + 1, w1, new)

    cown = own_ref[at_ref[10] + j]
    start = pl.multiple_of(j * B, B)
    o_ref[...] = w_ref[...] - dot(half_ref[...], q_ref[:, pl.ds(start, B)])

    @pl.when(cown > g)
    def _():
        for i in range(rb):
            rown = own_ref[at_ref[9] + i]

            @pl.when((rown == g) | ((rown == g + 1) & (cown > g + 1)))
            def _():
                o_ref[i * B : (i + 1) * B] = jnp.zeros((B, B), jnp.float32)

    for turn in range(PANELS):
        @pl.when(cown == g + turn)
        def _():
            for i in range(rb):
                span = slice(i * B, (i + 1) * B)
                rown = own_ref[at_ref[9] + i]

                @pl.when(rown > g + turn)
                def _():
                    o_ref[span] = full_ref[span, turn * B : (turn + 1) * B]

                @pl.when(rown == g + turn)
                def _():
                    o_ref[span] = f_ref[turn]


def tail(owner, at, w, cols, rowp, factors, z, x, everyone, v):
    rows, width = w.shape
    fixed = lambda rank, *at: (lambda j, a, b: tuple(at) if at else (0,) * rank)
    stripe = lambda j, a, b: (0, j)
    heads = everyone.shape[0] - 3 * B
    whole = lambda x: pl.BlockSpec(x.shape, fixed(x.ndim))
    return pl.pallas_call(
        functools.partial(tail_kernel, rb=rows // B, cb=width // B),
        grid_spec=pltpu.PrefetchScalarGridSpec(
            num_scalar_prefetch=2,
            grid=(width // B,),
            in_specs=[
                pl.BlockSpec((rows, B), stripe),
                whole(cols),
                whole(rowp),
                whole(factors),
                whole(z),
                whole(x),
                pl.BlockSpec((heads, B), fixed(2, 3 * B // heads, 0)),
                whole(v),
            ],
            out_specs=[pl.BlockSpec((rows, B), stripe), whole(v)],
            scratch_shapes=[
                pltpu.VMEM((2 * B, width), jnp.bfloat16),
                pltpu.VMEM((rows, 2 * B), jnp.float32),
                pltpu.VMEM((rows, 2 * B), jnp.bfloat16),
            ],
        ),
        out_shape=(jax.ShapeDtypeStruct(w.shape, w.dtype), jax.ShapeDtypeStruct(v.shape, v.dtype)),
    )(owner, at, w, cols, rowp, factors, z, x, everyone, v)


def prep_kernel(at_ref, wc_ref, wr_ref, cols_ref, rowp_ref):
    t = pl.program_id(0)
    cols_ref[...] = jnp.where(at_ref[4 + t] > 0, wc_ref[...], 0.0)
    rowp_ref[...] = jnp.where(at_ref[6 + t] > 0, wr_ref[...], 0.0).astype(jnp.bfloat16)


def prep(at, w):
    rows, width = w.shape
    return pl.pallas_call(
        prep_kernel,
        grid_spec=pltpu.PrefetchScalarGridSpec(
            num_scalar_prefetch=1,
            grid=(PANELS,),
            in_specs=[
                pl.BlockSpec((rows, B), lambda t, a: (0, a[t])),
                pl.BlockSpec((B, width), lambda t, a: (a[2 + t], 0)),
            ],
            out_specs=[
                pl.BlockSpec((rows, B), lambda t, a: (0, t)),
                pl.BlockSpec((B, width), lambda t, a: (t, 0)),
            ],
        ),
        out_shape=(
            jax.ShapeDtypeStruct((rows, PANELS * B), jnp.float32),
            jax.ShapeDtypeStruct((PANELS * B, width), jnp.bfloat16),
        ),
    )(at, w, w)


MESH = pl.DeviceIdType.MESH
CHUNKS = 32
LAG = 5


def remote(src, dst, send, recv, where):
    return pltpu.make_async_remote_copy(
        src_ref=src, dst_ref=dst, send_sem=send, recv_sem=recv, device_id=where, device_id_type=MESH
    )


class RowSpread:
    def __init__(self, axis_size, in_ref, acc_ref, core_ref, hop_ref, send, recv):
        self.bits = [1 << b for b in range(1, axis_size.bit_length() - 1)]
        self.in_ref, self.acc, self.core, self.hop = in_ref, acc_ref, core_ref, hop_ref
        self.send, self.recv = send, recv
        me = lax.axis_index("row")
        self.me = me
        self.odd = lax.rem(me, 2)
        self.mate = me + 1 - 2 * self.odd
        self.rows = in_ref.shape[0]
        self.half = self.rows // 2
        self.quarter = self.rows // 4
        self.stages = len(self.bits)

    def mine(self, part=0, size=None):
        start = self.odd * self.half + part * self.quarter
        return pl.ds(pl.multiple_of(start, self.quarter), self.half if size is None else size)

    def theirs(self):
        start = (1 - self.odd) * self.half
        return pl.ds(pl.multiple_of(start, self.half), self.half)

    def partner(self, bit):
        digit = lax.rem(self.me // bit, 2)
        return {"row": self.me + bit - 2 * bit * digit}

    def first(self):
        return remote(self.in_ref.at[self.theirs()], self.core, self.send.at[0], self.recv.at[0], {"row": self.mate})

    def middle(self, stage, part):
        bit = self.bits[(stage + part) % self.stages]
        index = 1 + 2 * stage + part
        return remote(
            self.acc.at[self.mine(part, self.quarter)],
            self.hop.at[stage, part],
            self.send.at[index],
            self.recv.at[index],
            self.partner(bit),
        )

    def final(self):
        index = 1 + 2 * self.stages
        rows = self.acc.at[self.mine()]
        return remote(rows, rows, self.send.at[index], self.recv.at[index], {"row": self.mate})

    def start(self):
        self.first().start()

    def advance(self, turn):
        if turn == 0:
            self.first().wait()
            self.acc[self.mine()] = self.in_ref[self.mine()] + self.core[...]
        else:
            for part in range(2):
                self.middle(turn - 1, part).wait()
                rows = self.mine(part, self.quarter)
                self.acc[rows] = self.acc[rows] + self.hop[turn - 1, part]
        if turn < self.stages:
            for part in range(2):
                self.middle(turn, part).start()
        else:
            self.final().start()

    def finish(self):
        self.final().wait()


def spread_scratch(axis_size, shape, dtype):
    stages = axis_size.bit_length() - 2
    rows, width = shape
    count = 2 + 2 * stages
    return [
        pltpu.VMEM((rows // 2, width), dtype),
        pltpu.VMEM((stages, 2, rows // 4, width), dtype),
        pltpu.SemaphoreType.DMA((count,)),
        pltpu.SemaphoreType.DMA((count,)),
    ]


def gather_kernel(
    nr, nc, own, rowp, inn, out, rowout, v,
    rin, lin, rtx, ltx, rs, rr, ls, lr,
    core, hop, rowsend, rowrecv, vsend, vrecv, vself,
):
    r = lax.axis_index("row")
    c = lax.axis_index("col")
    size = own.shape[0] // CHUNKS
    ratio = nr // nc
    spread = RowSpread(nr, rowp, rowout, core, hop, rowsend, rowrecv)
    part_p, width = inn.shape[1], inn.shape[2]

    def chunk(q):
        return pl.ds(pl.multiple_of(q * size, size), size)

    def right(src, q):
        return remote(src.at[chunk(q)], rin.at[chunk(q)], rs.at[q], rr.at[q], {"col": c + 1})

    def left(src, q):
        return remote(src.at[chunk(q)], lin.at[chunk(q)], ls.at[q], lr.at[q], {"col": c - 1})

    spread.start()

    @pl.when(c == 0)
    def _():
        lax.fori_loop(0, CHUNKS, lambda q, k: (right(own, q).start(), k)[1], 0)
        rin[...] = jnp.zeros_like(rin)

    @pl.when(c == nc - 1)
    def _():
        lax.fori_loop(0, CHUNKS, lambda q, k: (left(own, q).start(), k)[1], 0)
        lin[...] = jnp.zeros_like(lin)

    my_col = r // ratio

    def v_copy(group):
        place = v.at[
            pl.ds(pl.multiple_of(lax.rem(r, ratio) * part_p, part_p), part_p),
            pl.ds(pl.multiple_of(c * width, width), width),
        ]
        slot = lax.rem(r, ratio) * nc + c
        return remote(inn.at[group], place, vsend.at[group], vrecv.at[slot], {"row": group, "col": my_col})

    def v_local():
        place = v.at[
            pl.ds(pl.multiple_of(lax.rem(r, ratio) * part_p, part_p), part_p),
            pl.ds(pl.multiple_of(c * width, width), width),
        ]
        return pltpu.make_async_copy(inn.at[r], place, vself)

    for shift in range(nr):
        group = lax.rem(r + shift, nr)
        if shift == 0:
            @pl.when(my_col == c)
            def _():
                v_local().start()

            @pl.when(my_col != c)
            def _():
                v_copy(group).start()
        else:
            v_copy(group).start()

    steps = CHUNKS + LAG * (nc - 2)

    def relay(t, carry):
        q = t - LAG * (c - 1)

        @pl.when((c > 0) & (q >= 0) & (q < CHUNKS))
        def _():
            right(own, q).wait_recv()

            @pl.when(c < nc - 1)
            def _():
                rtx[chunk(q)] = rin[chunk(q)] + own[chunk(q)]
                right(rtx, q).start()

        p = t - LAG * (nc - 2 - c)

        @pl.when((c < nc - 1) & (p >= 0) & (p < CHUNKS))
        def _():
            left(own, p).wait_recv()

            @pl.when(c > 0)
            def _():
                ltx[chunk(p)] = lin[chunk(p)] + own[chunk(p)]
                left(ltx, p).start()

        return carry

    turns = spread.stages + 1
    begin = 0
    for turn in range(turns):
        end = 1 + (steps - 1) * (turn + 1) // (turns + 1)
        lax.fori_loop(begin, end, relay, 0)
        begin = end
        spread.advance(turn)
    lax.fori_loop(begin, steps, relay, 0)

    def total(q, carry):
        out[chunk(q)] = own[chunk(q)] + (rin[chunk(q)] + lin[chunk(q)])
        return carry

    lax.fori_loop(0, CHUNKS, total, 0)

    @pl.when(c < nc - 1)
    def _():
        lax.fori_loop(0, CHUNKS, lambda q, k: (right(own, q).wait_send(), k)[1], 0)

    @pl.when(c > 0)
    def _():
        lax.fori_loop(0, CHUNKS, lambda q, k: (left(own, q).wait_send(), k)[1], 0)

    spread.finish()
    for shift in range(nr):
        group = lax.rem(r + shift, nr)
        if shift == 0:
            @pl.when(my_col == c)
            def _():
                v_local().wait()

            @pl.when(my_col != c)
            def _():
                v_copy(group).wait_send()
        else:
            v_copy(group).wait_send()
    for a in range(ratio):
        for b in range(nc):
            @pl.when((r != ratio * c + a) | (c != b))
            def _():
                place = v.at[pl.ds(a * part_p, part_p), pl.ds(b * width, width)]
                remote(
                    inn.at[0], place, vsend.at[0], vrecv.at[a * nc + b], {"row": r, "col": c}
                ).wait_recv()


def gather(nr, nc, own, rowp, inn):
    rows, width = own.shape
    vmem = pl.BlockSpec(memory_space=pltpu.VMEM)
    ratio = nr // nc
    big = pltpu.VMEM((rows, width), jnp.float32)
    sems = pltpu.SemaphoreType.DMA((CHUNKS,))
    return pl.pallas_call(
        functools.partial(gather_kernel, nr, nc),
        out_shape=(
            jax.ShapeDtypeStruct(own.shape, own.dtype),
            jax.ShapeDtypeStruct(rowp.shape, rowp.dtype),
            jax.ShapeDtypeStruct((ratio * inn.shape[1], nc * inn.shape[2]), inn.dtype),
        ),
        in_specs=[vmem] * 3,
        out_specs=(vmem,) * 3,
        scratch_shapes=[big] * 4 + [sems] * 4
        + spread_scratch(nr, rowp.shape, rowp.dtype)
        + [
            pltpu.SemaphoreType.DMA((nr,)),
            pltpu.SemaphoreType.DMA((ratio * nc,)),
            pltpu.SemaphoreType.DMA,
        ],
        compiler_params=pltpu.CompilerParams(has_side_effects=True),
    )(own, rowp, inn)


def spread_kernel(nr, in_ref, out_ref, core, hop, send, recv):
    spread = RowSpread(nr, in_ref, out_ref, core, hop, send, recv)
    spread.start()
    for turn in range(spread.stages + 1):
        spread.advance(turn)
    spread.finish()


def spread_rows(nr, value):
    vmem = pl.BlockSpec(memory_space=pltpu.VMEM)
    return pl.pallas_call(
        functools.partial(spread_kernel, nr),
        out_shape=jax.ShapeDtypeStruct(value.shape, value.dtype),
        in_specs=[vmem],
        out_specs=vmem,
        scratch_shapes=spread_scratch(nr, value.shape, value.dtype),
        compiler_params=pltpu.CompilerParams(has_side_effects=True),
    )(value)


def per_device(covariance, innovations, block_owner, panel_index):
    local_rows, local_cols = covariance.shape
    row_blocks = local_rows // B
    column_blocks = local_cols // B
    r_here = lax.axis_index("row")
    c_here = lax.axis_index("col")
    nr, nc = lax.axis_size("row"), lax.axis_size("col")
    g = panel_index[0]
    index = jnp.arange(12, dtype=jnp.int32)
    positions = jnp.arange(block_owner.shape[0], dtype=jnp.int32)
    match = block_owner[None, :] == (panel_index[0] + index % PANELS)[:, None]
    slot = jnp.sum(jnp.where(match, positions[None, :], 0), axis=1)
    options = [
        slot % column_blocks,
        slot % row_blocks,
        (slot // column_blocks == c_here).astype(jnp.int32),
        (slot // row_blocks == r_here).astype(jnp.int32),
        jnp.where(index % PANELS == 0, g, r_here * row_blocks),
    ]
    places = c_here * column_blocks
    for kind, option in reversed(list(enumerate(options))):
        places = jnp.where(index // PANELS == kind, option, places)
    places = places.astype(jnp.int32)
    cols, rowpanel = prep(places, covariance)
    cols, rowpanel, v = gather(nr, nc, cols, rowpanel, innovations.transpose(1, 0, 2))

    def pick(value, t, axis):
        tile = lax.dynamic_slice_in_dim(value, places[2 + t] * B, B, axis)
        return jnp.where(places[6 + t] > 0, tile, 0.0)

    parts = [pick(cols[:, :B], 0, 0), pick(cols[:, :B], 1, 0), pick(cols[:, B:], 1, 0), pick(v, 0, 1), pick(v, 1, 1)]
    everyone = spread_rows(nr, jnp.concatenate(parts, axis=0))
    factors, z, x = factor_pair(everyone)
    return tail(block_owner, places, covariance, cols, rowpanel, factors, z, x, everyone, v)


def solution(mesh):
    placed = (P("row", "col"), P("row", None, "col"), P(), P())
    return jax.shard_map(
        per_device,
        mesh=mesh,
        in_specs=placed,
        out_specs=(P("row", "col"), P("col", "row")),
        check_vma=False,
    )
```
